128 devices in a mesh: wide: 32 (over y, x, core), narrow: 4 (over z).
Axes of the slice: x: 4, y: 4, z: 4, core: 2. Of those that a mesh axis runs over, the one named last changes fastest.
Arguments:
- slab: float32 [96, 512, 8192], P('narrow', 'wide'), may hold values from -24 to 24, as said below
- start: float32 [512, 64], replicated, may hold values from -6 to 6
Outputs:
- core: float32 [96, 64, 8192], P('narrow', None, 'wide')
- factor: float32 [512, 64], replicated
The draws below stay inside these ranges and needn't reach their ends.
Inputs may be any that keep to these rules, and one draw needn't show every extreme that they name: The slab is a planted sum of 64 separable terms plus noise.
All inputs are finite; a program needn't handle non-finite values.
Results may differ from the reference program's by a relative error of at most 0.0003.
Values sent between devices are 32-bit elements; how exact they have to be, the bound alone decides.
A program may use at most 256 MiB of HBM per device.

```python
import jax
import jax.numpy as jnp
from jax import lax

F1 = 512
F2 = 8192
RANK = 64
ITERS = 2
SPECTRA = 96


def draw_slab(key, part):
    keys = jax.random.split(jax.random.fold_in(key, 11), 5)
    left = jax.random.normal(keys[0], (F1, RANK), jnp.float32)
    spread = jnp.exp(jax.random.uniform(keys[1], (RANK,), jnp.float32, 0.0, 1.0986))
    right = jax.random.normal(keys[2], (SPECTRA, RANK, F2), jnp.float32) * (spread / RANK ** 0.5)[None, :, None]
    planted = jnp.einsum('ik,skf->sif', left, right, precision=lax.Precision.HIGHEST)
    noise = 0.7 * jax.random.normal(keys[4], (SPECTRA, F1, F2), jnp.float32)
    return jnp.clip(planted + noise, -24.0, 24.0)


def centred(key, extent, scale, limit, dtype=jnp.bfloat16):
    result = jax.random.normal(key, extent, jnp.float32) * scale
    return jnp.minimum(jnp.maximum(result, -limit), limit).astype(dtype)


def setup_inputs(seed: int = 0) -> dict:
    arg_keys = jax.random.split(jax.random.key(seed), 3)
    slab = draw_slab(jax.random.fold_in(arg_keys[2], 71), 0)
    start = centred(arg_keys[1], (F1, RANK), 1.0, 6.0, jnp.float32)
    return {"slab": slab, "start": start}


def orthonormal(matrix):
    product = jnp.dot(matrix.T, matrix, precision=lax.Precision.HIGHEST)
    lower = jnp.linalg.cholesky(product)
    return lax.linalg.triangular_solve(lower, matrix, left_side=False, lower=True, transpose_a=True)

def reference(slab, start):
    gram = jnp.einsum('sif,sjf->ij', slab, slab, precision=lax.Precision.HIGHEST)
    basis = orthonormal(start)
    for step in range(ITERS):
        basis = orthonormal(jnp.dot(gram, basis, precision=lax.Precision.HIGHEST))
    core = jnp.einsum('ik,sif->skf', basis, slab, precision=lax.Precision.HIGHEST)
    return (core, basis)
```

```python
import jax
import jax.numpy as jnp
from jax import lax
from jax.experimental import pallas as pl
from jax.experimental.pallas import tpu as pltpu
from jax.sharding import PartitionSpec as P

MESH = pl.DeviceIdType.MESH
F32, BF16 = jnp.float32, jnp.bfloat16
ITERS = 2
NX, NY, CORES, NZ = 4, 4, 2, 4
WIDE = NX * NY * CORES
PEERS = [(y, x, c) for y in range(NY) for x in range(NX) for c in range(CORES) if (y, x, c) != (0, 0, 0)]


def dot(a, b, dims=((1,), (0,)), exact=True):
    precision = lax.Precision.HIGHEST if exact else None
    return lax.dot_general(a, b, (dims, ((), ())), precision=precision, preferred_element_type=F32)


def split(x):
    high = x.astype(BF16)
    return high, (x - high.astype(F32)).astype(BF16)


def inverse_factor(gram2):
    n = gram2.shape[0]
    row = lax.broadcasted_iota(jnp.int32, (n, 2 * n), 0)
    lane = lax.broadcasted_iota(jnp.int32, (n, 2 * n), 1)
    work = jnp.where(lane < n, jnp.concatenate([gram2, gram2], axis=1), (lane - n == row).astype(F32))

    def step(k, work):
        pivot_row = jnp.sum(jnp.where(row == k, work, 0.0), axis=0, keepdims=True)
        column = jnp.sum(jnp.where(lane == k, work, 0.0), axis=1, keepdims=True)
        pivot = jnp.sum(jnp.where(lane[:1] == k, pivot_row, 0.0), axis=1, keepdims=True)
        scale = 1.0 / jnp.sqrt(pivot)
        scaled = pivot_row * scale
        return jnp.where(row == k, scaled, jnp.where(row > k, work - (column * scale) * scaled, work))

    work = lax.fori_loop(0, n, step, work)
    return work[:, n:]


def orthonormal(zp):
    both = dot(zp, zp, ((0,), (0,)))
    inv_t = inverse_factor(both[:64, :64] + both[64:, 64:]).T
    zero = jnp.zeros_like(inv_t)
    blocks = jnp.concatenate(
        [jnp.concatenate([inv_t, zero], axis=1), jnp.concatenate([zero, inv_t], axis=1)], axis=0)
    return dot(zp, blocks)


def kernel(x_ref, start_ref, core_ref, factor_ref, buf, high, low, gram, out_buf, zsend, zslots, zz, zall,
           own_sem, send_sem, recv_sem, out_sem, zsend_sem, rs_sem, zz_send_sem, zz_sem, ag_send_sem, ag_sem):
    w = lax.axis_index("wide")
    z = lax.axis_index("narrow")
    cc, xx, yy = lax.rem(w, CORES), lax.rem(w // CORES, NX), w // (CORES * NX)
    spectra, rows, cols = buf.shape[0], x_ref.shape[1], buf.shape[2]

    def peer(offset):
        y, x, c = offset
        return (lax.rem(yy + y, NY) * NX + lax.rem(xx + x, NX)) * CORES + lax.rem(cc + c, CORES)

    peers = [peer(offset) for offset in PEERS]
    depths = [lax.rem(z + d, NZ) for d in range(1, NZ)]

    barrier = pltpu.get_barrier_semaphore()
    for t in peers:
        pl.semaphore_signal(barrier, inc=1, device_id=(t, z), device_id_type=MESH)
    for d in depths:
        pl.semaphore_signal(barrier, inc=1, device_id=(w, d), device_id_type=MESH)
    pl.semaphore_wait(barrier, len(peers) + len(depths))

    def block(ref, t):
        return ref.at[:, pl.ds(pl.multiple_of(t * cols, cols), cols)]

    my_rows = pl.ds(pl.multiple_of(w * rows, rows), rows)

    @pl.loop(0, spectra)
    def _(s):
        for t in peers:
            pltpu.make_async_remote_copy(
                src_ref=block(x_ref.at[s], t), dst_ref=buf.at[s, my_rows, :],
                send_sem=send_sem, recv_sem=recv_sem.at[s], device_id=(t, z), device_id_type=MESH).start()

    own = pltpu.make_async_copy(
        x_ref.at[:, :, pl.ds(pl.multiple_of(w * cols, cols), cols)], buf.at[:, my_rows, :], own_sem)
    own.start()

    start = start_ref[...]
    basis = orthonormal(jnp.concatenate([start[:256], start[256:]], axis=1))
    gram[...] = jnp.zeros_like(gram)
    own.wait()

    def arrived(ref, sem):
        pltpu.make_async_copy(ref, ref, sem).wait()

    @pl.loop(0, spectra)
    def _(s):
        arrived(buf.at[s, pl.ds(0, len(PEERS) * rows), :], recv_sem.at[s])
        h, l = split(buf[s])
        high[s] = h
        low[s] = l
        nt = ((1,), (1,))
        gram[...] += (dot(h, h, nt, False) + dot(h, l, nt, False)) + (dot(l, h, nt, False) + dot(l, l, nt, False))

    for it in range(ITERS):
        top, bottom = basis[:, :64], basis[:, 64:]
        parts = [dot(gram[pl.ds(r, 256), pl.ds(0, 256)], top) + dot(gram[pl.ds(r, 256), pl.ds(256, 256)], bottom)
                 for r in (0, 256)]
        zsend[it] = jnp.concatenate(parts, axis=1)
        for t in peers:
            pltpu.make_async_remote_copy(
                src_ref=zsend.at[it, pl.ds(pl.multiple_of(t * 8, 8), 8), :], dst_ref=zslots.at[it, w],
                send_sem=zsend_sem.at[it], recv_sem=rs_sem.at[it], device_id=(t, z), device_id_type=MESH).start()
        zslots[it, w] = zsend[it, pl.ds(pl.multiple_of(w * 8, 8), 8), :]
        arrived(zslots.at[it, pl.ds(0, len(PEERS))], rs_sem.at[it])
        zz[it, z] = jnp.sum(zslots[it], axis=0)
        for d in depths:
            pltpu.make_async_remote_copy(
                src_ref=zz.at[it, z], dst_ref=zz.at[it, z],
                send_sem=zz_send_sem.at[it], recv_sem=zz_sem.at[it], device_id=(w, d), device_id_type=MESH).start()
        arrived(zz.at[it, pl.ds(0, len(depths))], zz_sem.at[it])
        mine = pl.ds(pl.multiple_of(w * 8, 8), 8)
        zall[it, mine, :] = (zz[it, 0] + zz[it, 1]) + (zz[it, 2] + zz[it, 3])
        for t in peers:
            pltpu.make_async_remote_copy(
                src_ref=zall.at[it, mine, :], dst_ref=zall.at[it, mine, :],
                send_sem=ag_send_sem.at[it], recv_sem=ag_sem.at[it], device_id=(t, z), device_id_type=MESH).start()
        arrived(zall.at[it, pl.ds(0, len(PEERS) * 8), :], ag_sem.at[it])
        basis = orthonormal(zall[it])

    factor_ref[0:256, :] = basis[:, :64]
    factor_ref[256:512, :] = basis[:, 64:]
    basis_t = basis.T
    bh, bl = split(jnp.concatenate([basis_t[:64], basis_t[64:]], axis=1))
    both = jnp.concatenate([bh, bl], axis=0)

    @pl.loop(0, spectra)
    def _(s):
        wide = dot(both, high[s], exact=False)
        out_buf[s] = (wide[:64] + wide[64:]) + dot(bh, low[s], exact=False)
        pltpu.make_async_copy(out_buf.at[s], core_ref.at[s], out_sem).start()

    arrived(buf.at[:, pl.ds(0, len(PEERS) * rows), :], send_sem)
    for it in range(ITERS):
        arrived(zslots.at[it, pl.ds(0, len(PEERS))], zsend_sem.at[it])
        arrived(zz.at[it, pl.ds(0, len(depths))], zz_send_sem.at[it])
        arrived(zall.at[it, pl.ds(0, len(PEERS) * 8), :], ag_send_sem.at[it])
    arrived(out_buf, out_sem)


def on_device(slab, start):
    spectra, rows, columns = slab.shape
    cols = columns // WIDE
    dma = pltpu.SemaphoreType.DMA
    return pl.pallas_call(
        kernel,
        out_shape=(jax.ShapeDtypeStruct((spectra, 64, cols), F32), jax.ShapeDtypeStruct((512, 64), F32)),
        in_specs=[pl.BlockSpec(memory_space=pltpu.HBM), pl.BlockSpec(memory_space=pltpu.VMEM)],
        out_specs=(pl.BlockSpec(memory_space=pltpu.HBM), pl.BlockSpec(memory_space=pltpu.VMEM)),
        scratch_shapes=[
            pltpu.VMEM((spectra, 512, cols), F32),
            pltpu.VMEM((spectra, 512, cols), BF16),
            pltpu.VMEM((spectra, 512, cols), BF16),
            pltpu.VMEM((512, 512), F32),
            pltpu.VMEM((spectra, 64, cols), F32),
            pltpu.VMEM((ITERS, 256, 128), F32),
            pltpu.VMEM((ITERS, WIDE, 8, 128), F32),
            pltpu.VMEM((ITERS, NZ, 8, 128), F32),
            pltpu.VMEM((ITERS, 256, 128), F32),
            dma(()), dma(()), dma((spectra,)), dma(()),
            dma((ITERS,)), dma((ITERS,)), dma((ITERS,)), dma((ITERS,)), dma((ITERS,)), dma((ITERS,)),
        ],
        compiler_params=pltpu.CompilerParams(
            collective_id=0, has_side_effects=True, vmem_limit_bytes=56 * 2**20),
    )(slab, start)


def solution(mesh):
    return jax.shard_map(
        on_device,
        mesh=mesh,
        in_specs=(P("narrow", "wide", None), P()),
        out_specs=(P("narrow", None, "wide"), P()),
        check_vma=False,
    )
```

```python
import jax
import jax.numpy as jnp
from jax import lax
from jax.experimental import pallas as pl
from jax.experimental.pallas import tpu as pltpu
from jax.sharding import PartitionSpec as P

MESH = pl.DeviceIdType.MESH
F32, BF16 = jnp.float32, jnp.bfloat16
ITERS = 2
AHEAD = 8
PARTS = 2
GROUP = 8
KERNEL_VMEM = 40 * 2**20
PROJECT_VMEM = 8 * 2**20
NX, NY, CORES, NZ = 4, 4, 2, 4
WIDE = NX * NY * CORES
PEERS = [(y, x, c) for y in range(NY) for x in range(NX) for c in range(CORES) if (y, x, c) != (0, 0, 0)]


def dot(a, b, dims=((1,), (0,)), exact=True):
    precision = lax.Precision.HIGHEST if exact else None
    return lax.dot_general(a, b, (dims, ((), ())), precision=precision, preferred_element_type=F32)


def split(x):
    high = x.astype(BF16)
    return high, (x - high.astype(F32)).astype(BF16)


def inverse_factor(gram2):
    n = gram2.shape[0]
    sub = lax.broadcasted_iota(jnp.int32, (8, 2 * n), 0)
    lane = lax.broadcasted_iota(jnp.int32, (8, 2 * n), 1)
    doubled = jnp.concatenate([gram2, gram2], axis=1)
    work = [jnp.where(lane < n, doubled[8 * i:8 * i + 8], (lane - n == sub + 8 * i).astype(F32)) for i in range(n // 8)]

    def spread(x):
        return jnp.broadcast_to(x, (8, 2 * n))

    for k in range(0, n, 4):
        b, j = divmod(k, 8)
        pivot = work[b]
        r = [spread(pivot[j + t:j + t + 1]) for t in range(4)]
        e = [[spread(pivot[j + t:j + t + 1, k + u:k + u + 1]) for u in range(t + 1)] for t in range(4)]
        inv0 = 1.0 / (e[0][0] * e[1][1] - e[1][0] * e[1][0])
        y0 = (e[1][1] * r[0] - e[1][0] * r[1]) * inv0
        y1 = (e[0][0] * r[1] - e[1][0] * r[0]) * inv0
        r2 = r[2] - (e[2][0] * y0 + e[2][1] * y1)
        r3 = r[3] - (e[3][0] * y0 + e[3][1] * y1)

        def reduced(t, u):
            return e[t][u] - (e[1][1] * e[u][0] * e[t][0] - e[1][0] * (e[u][1] * e[t][0] + e[u][0] * e[t][1])
                              + e[0][0] * e[u][1] * e[t][1]) * inv0

        p, q, v = reduced(2, 2), reduced(3, 2), reduced(3, 3)
        inv1 = 1.0 / (p * v - q * q)
        y2 = (v * r2 - q * r3) * inv1
        y3 = (p * r3 - q * r2) * inv1
        f = [[spread(y[:1, k + t:k + t + 1]) for y in (y0, y1)] for t in (2, 3)]
        work[b] = jnp.where(sub == j + 2, r2, jnp.where(sub == j + 3, r3, pivot))
        for i in range(b, n // 8):
            if i == b and j == 4:
                continue
            source = pivot if i == b else work[i]
            c = [spread(source[:, k + t:k + t + 1]) for t in range(4)]
            c2 = c[2] - (c[0] * f[0][0] + c[1] * f[0][1])
            c3 = c[3] - (c[0] * f[1][0] + c[1] * f[1][1])
            update = (c[0] * y0 + c[1] * y1) + (c2 * y2 + c3 * y3)
            work[i] = work[i] - (jnp.where(sub > j + 3, update, 0.0) if i == b else update)

    odd = sub % 2 == 1
    rows = []
    for i in range(n // 8):
        first = sub - sub % 2 + 8 * i
        before = jnp.concatenate([work[i][7:8], work[i][:7]], axis=0)
        here = jnp.where(lane == first, work[i], 0.0)
        q = jnp.sum(jnp.where(odd, here, 0.0), axis=1, keepdims=True)
        p = jnp.sum(jnp.where(odd, jnp.where(lane == first, before, 0.0), here), axis=1, keepdims=True)
        v = jnp.sum(jnp.where(jnp.logical_and(odd, lane == first + 1), work[i], 0.0), axis=1, keepdims=True)
        m = q / p
        rows.append((work[i] - m * before) / jnp.sqrt(jnp.where(odd[:, :1], v - q * m, p)))
    return jnp.concatenate(rows, axis=0)[:, n:]


def inverse_of(zt):
    c = dot(zt, zt, ((1,), (1,)))
    n = c.shape[0]
    on = lax.broadcasted_iota(jnp.int32, (n, n), 0) == lax.broadcasted_iota(jnp.int32, (n, n), 1)
    diagonal = jnp.where(on, c, 0.0)
    down = 1.0 / jnp.sqrt(jnp.sum(diagonal, axis=1, keepdims=True))
    across = 1.0 / jnp.sqrt(jnp.sum(diagonal, axis=0, keepdims=True))
    return inverse_factor((c * down) * across) * across


def fold(stacked):
    return stacked[:64] + stacked[64:]


def split3(x):
    high = x.astype(BF16)
    rest = x - high.astype(F32)
    middle = rest.astype(BF16)
    return high, middle, (rest - middle.astype(F32)).astype(BF16)


def kernel(x_ref, start_ref, high, low, basis_ref, start_buf, buf, gram, pair, zacc, g3, zsend, zslots, zz, zall,
           start_sem, own_sem, send_sem, recv_sem, zsend_sem, rs_sem, zz_send_sem, zz_sem, ag_send_sem, ag_sem):
    w = lax.axis_index("wide")
    z = lax.axis_index("narrow")
    cc, xx, yy = lax.rem(w, CORES), lax.rem(w // CORES, NX), w // (CORES * NX)
    spectra, rows, cols = buf.shape[0], x_ref.shape[1], buf.shape[2]

    def peer(offset):
        y, x, c = offset
        return (lax.rem(yy + y, NY) * NX + lax.rem(xx + x, NX)) * CORES + lax.rem(cc + c, CORES)

    peers = [peer(offset) for offset in PEERS]
    far_first = [peer(offset) for offset in sorted(PEERS, key=lambda o: -min(o[0], NY - o[0]) - min(o[1], NX - o[1]))]
    depths = [lax.rem(z + d, NZ) for d in (2, 1, 3)]

    barrier = pltpu.get_barrier_semaphore()
    for t in far_first:
        pl.semaphore_signal(barrier, inc=1, device_id=(t, z), device_id_type=MESH)
    for d in depths:
        pl.semaphore_signal(barrier, inc=1, device_id=(w, d), device_id_type=MESH)
    my_rows = pl.ds(pl.multiple_of(w * rows, rows), rows)
    own = pltpu.make_async_copy(
        x_ref.at[:, :, pl.ds(pl.multiple_of(w * cols, cols), cols)], buf.at[:, my_rows, :], own_sem)
    own.start()
    begun = pltpu.make_async_copy(start_ref, start_buf, start_sem)
    begun.start()
    pl.semaphore_wait(barrier, len(peers) + len(depths))

    part = rows // PARTS

    def send(s):
        for r in range(PARTS):
            here = pl.ds(pl.multiple_of(w * rows + r * part, part), part)
            for t in peers:
                pltpu.make_async_remote_copy(
                    src_ref=x_ref.at[s, pl.ds(r * part, part), pl.ds(pl.multiple_of(t * cols, cols), cols)],
                    dst_ref=buf.at[s, here, :],
                    send_sem=send_sem, recv_sem=recv_sem.at[s], device_id=(t, z), device_id_type=MESH).start()

    def arrived(ref, sem):
        pltpu.make_async_copy(ref, ref, sem).wait()

    nt = ((1,), (1,))

    def multiply(s):
        arrived(buf.at[s, pl.ds(0, len(PEERS) * rows), :], recv_sem.at[s])
        h, l = split(buf[s])
        high[s] = h
        low[s] = l
        inner = jnp.concatenate(split(fold(dot(pair[...], h, exact=False) + dot(pair[...], l, exact=False))), axis=0)
        zacc[...] += fold(dot(inner, h, nt, False) + dot(inner, l, nt, False))

    def accumulate(s):
        h, l = high[s], low[s]
        gram[...] += (dot(h, h, nt, False) + dot(h, l, nt, False)) + (dot(l, h, nt, False) + dot(l, l, nt, False))

    @pl.loop(0, AHEAD)
    def _(s):
        send(s)

    gram[...] = jnp.zeros_like(gram)
    zacc[...] = jnp.zeros_like(zacc)
    begun.wait()
    start = start_buf[...]
    pair[...] = jnp.concatenate(split(dot(inverse_of(start), start)), axis=0)
    own.wait()

    @pl.loop(0, spectra - AHEAD)
    def _(s):
        send(s + AHEAD)
        multiply(s)
        accumulate(s)

    @pl.loop(spectra - AHEAD, spectra - 1)
    def _(s):
        multiply(s)
        accumulate(s)

    multiply(spectra - 1)

    def tile(ref, t):
        return ref.at[pl.ds(pl.multiple_of(t // 4 * 8, 8), 8), pl.ds(pl.multiple_of(lax.rem(t, 4) * 128, 128), 128)]

    def reduce(it, value):
        zsend[it] = value
        for t in far_first:
            pltpu.make_async_remote_copy(
                src_ref=tile(zsend.at[it], t), dst_ref=zslots.at[it, w],
                send_sem=zsend_sem.at[it], recv_sem=rs_sem.at[it], device_id=(t, z), device_id_type=MESH).start()
        zslots[it, w] = tile(zsend.at[it], w)[...]

    def spread(it):
        arrived(zslots.at[it, pl.ds(0, len(PEERS))], rs_sem.at[it])
        zz[it, z] = jnp.sum(zslots[it], axis=0)
        for d in depths:
            pltpu.make_async_remote_copy(
                src_ref=zz.at[it, z], dst_ref=zz.at[it, z],
                send_sem=zz_send_sem.at[it], recv_sem=zz_sem.at[it], device_id=(w, d), device_id_type=MESH).start()
        arrived(zz.at[it, pl.ds(0, len(depths))], zz_sem.at[it])
        tile(zall.at[it], w)[...] = (zz[it, 0] + zz[it, 1]) + (zz[it, 2] + zz[it, 3])
        for t in far_first:
            pltpu.make_async_remote_copy(
                src_ref=tile(zall.at[it], w), dst_ref=tile(zall.at[it], w),
                send_sem=ag_send_sem.at[it], recv_sem=ag_sem.at[it], device_id=(t, z), device_id_type=MESH).start()

    def gathered(it):
        arrived(zslots.at[it, pl.ds(0, len(PEERS))], ag_sem.at[it])
        return zall[it]

    reduce(0, zacc[...])
    accumulate(spectra - 1)
    for i, g in enumerate(split3(gram[...])):
        g3[i] = g
    spread(0)
    z1 = gathered(0)
    zh, zm, zl = split3(z1)
    by_high = dot(jnp.concatenate([zh, zm, zl], axis=0), g3[0], exact=False)
    by_middle = dot(jnp.concatenate([zh, zm], axis=0), g3[1], exact=False)
    by_low = dot(zh, g3[2], exact=False)
    reduce(1, by_high[:64] + ((by_high[64:128] + by_middle[:64]) + ((by_high[128:] + by_middle[64:]) + by_low)))
    inv1 = inverse_of(z1)
    spread(1)
    z2 = dot(inv1, gathered(1))
    basis_ref[...] = dot(inverse_of(z2), z2)

    arrived(buf.at[:, pl.ds(0, len(PEERS) * rows), :], send_sem)
    for it in range(ITERS):
        arrived(zslots.at[it, pl.ds(0, len(PEERS))], zsend_sem.at[it])
        arrived(zz.at[it, pl.ds(0, len(depths))], zz_send_sem.at[it])
        arrived(zslots.at[it, pl.ds(0, len(PEERS))], ag_send_sem.at[it])


def project(high, low, basis_ref, core_ref, factor_ref):
    basis = basis_ref[...]
    bh, bl = split(basis)
    both = jnp.concatenate([bh, bl], axis=0)
    step = pl.program_id(0)

    @pl.when(step == 0)
    def _():
        factor_ref[...] = basis

    for i in range(core_ref.shape[0]):
        s = step * core_ref.shape[0] + i
        core_ref[i] = fold(dot(both, high[s], exact=False)) + dot(bh, low[s], exact=False)


def on_device(slab, start):
    spectra, rows, columns = slab.shape
    cols = columns // WIDE
    dma = pltpu.SemaphoreType.DMA
    vmem = pl.BlockSpec(memory_space=pltpu.VMEM)
    hbm = pl.BlockSpec(memory_space=pltpu.HBM)
    high, low, basis = pl.pallas_call(
        kernel,
        out_shape=(pltpu.VMEM((spectra, 512, cols), BF16), pltpu.VMEM((spectra, 512, cols), BF16),
                   pltpu.VMEM((64, 512), F32)),
        in_specs=[hbm, hbm],
        out_specs=(vmem, vmem, vmem),
        scratch_shapes=[
            pltpu.VMEM((64, 512), F32),
            pltpu.VMEM((spectra, 512, cols), F32),
            pltpu.VMEM((512, 512), F32),
            pltpu.VMEM((128, 512), BF16),
            pltpu.VMEM((64, 512), F32),
            pltpu.VMEM((3, 512, 512), BF16),
            pltpu.VMEM((ITERS, 64, 512), F32),
            pltpu.VMEM((ITERS, WIDE, 8, 128), F32),
            pltpu.VMEM((ITERS, NZ, 8, 128), F32),
            pltpu.VMEM((ITERS, 64, 512), F32),
            dma(()), dma(()), dma(()), dma((spectra,)),
            dma((ITERS,)), dma((ITERS,)), dma((ITERS,)), dma((ITERS,)), dma((ITERS,)), dma((ITERS,)),
        ],
        compiler_params=pltpu.CompilerParams(
            collective_id=0, has_side_effects=True, vmem_limit_bytes=KERNEL_VMEM),
    )(slab, start.T)
    core, factor_t = pl.pallas_call(
        project,
        grid=(spectra // GROUP,),
        out_shape=(jax.ShapeDtypeStruct((spectra, 64, cols), F32), jax.ShapeDtypeStruct((64, 512), F32)),
        in_specs=[vmem, vmem, vmem],
        out_specs=(pl.BlockSpec((GROUP, 64, cols), lambda g: (g, 0, 0)), pl.BlockSpec((64, 512), lambda g: (0, 0))),
        compiler_params=pltpu.CompilerParams(vmem_limit_bytes=PROJECT_VMEM),
    )(high, low, basis)
    return core, factor_t.T


def solution(mesh):
    return jax.shard_map(
        on_device,
        mesh=mesh,
        in_specs=(P("narrow", "wide", None), P()),
        out_specs=(P("narrow", None, "wide"), P()),
        check_vma=False,
    )
```

```python
import jax
import jax.numpy as jnp
from jax import lax
from jax.experimental import pallas as pl
from jax.experimental.pallas import tpu as pltpu
from jax.sharding import PartitionSpec as P

MESH = pl.DeviceIdType.MESH
F32, BF16 = jnp.float32, jnp.bfloat16
ITERS = 2
AHEAD = 8
PARTS = 2
GROUP = 8
KERNEL_VMEM = 52953088
PROJECT_VMEM = 8 * 2**20
NX, NY, CORES, NZ = 4, 4, 2, 4
WIDE = NX * NY * CORES
PEERS = [(y, x, c) for y in range(NY) for x in range(NX) for c in range(CORES) if (y, x, c) != (0, 0, 0)]


def dot(a, b, dims=((1,), (0,)), exact=True):
    precision = lax.Precision.HIGHEST if exact else None
    return lax.dot_general(a, b, (dims, ((), ())), precision=precision, preferred_element_type=F32)


def split(x):
    high = x.astype(BF16)
    return high, (x - high.astype(F32)).astype(BF16)


def inverse_factor(gram2):
    n = gram2.shape[0]
    sub = lax.broadcasted_iota(jnp.int32, (8, 2 * n), 0)
    lane = lax.broadcasted_iota(jnp.int32, (8, 2 * n), 1)
    doubled = jnp.concatenate([gram2, gram2], axis=1)
    work = [jnp.where(lane < n, doubled[8 * i:8 * i + 8], (lane - n == sub + 8 * i).astype(F32)) for i in range(n // 8)]

    def spread(x):
        return jnp.broadcast_to(x, (8, 2 * n))

    for b in range(n // 8):
        k = 8 * b
        later = range(b + 1, n // 8)
        row = [spread(work[b][t:t + 1]) for t in range(8)]
        e = [[spread(work[b][t:t + 1, k + u:k + u + 1]) for u in range(t + 1)] for t in range(8)]
        column = {i: [spread(work[i][:, k + u:k + u + 1]) for u in range(8)] for i in later}
        update = {i: 0.0 for i in later}
        for p in range(0, 8, 2):
            aa, ab, bb = e[p][p], e[p + 1][p], e[p + 1][p + 1]
            inv = 1.0 / (aa * bb - ab * ab)
            y0 = (bb * row[p] - ab * row[p + 1]) * inv
            y1 = (aa * row[p + 1] - ab * row[p]) * inv
            f = {t: ((bb * e[t][p] - ab * e[t][p + 1]) * inv, (aa * e[t][p + 1] - ab * e[t][p]) * inv)
                 for t in range(p + 2, 8)}
            for i in later:
                update[i] = update[i] + (column[i][p] * y0 + column[i][p + 1] * y1)
                for t in range(p + 2, 8):
                    column[i][t] = column[i][t] - (column[i][p] * f[t][0] + column[i][p + 1] * f[t][1])
            for t in range(p + 2, 8):
                row[t] = row[t] - (e[t][p] * y0 + e[t][p + 1] * y1)
                for u in range(p + 2, t + 1):
                    e[t][u] = e[t][u] - (e[t][p] * f[u][0] + e[t][p + 1] * f[u][1])
        for t in range(2, 8):
            work[b] = jnp.where(sub == t, row[t], work[b])
        for i in later:
            work[i] = work[i] - update[i]

    odd = sub % 2 == 1
    rows = []
    for i in range(n // 8):
        first = sub - sub % 2 + 8 * i
        before = jnp.concatenate([work[i][7:8], work[i][:7]], axis=0)
        here = jnp.where(lane == first, work[i], 0.0)
        q = jnp.sum(jnp.where(odd, here, 0.0), axis=1, keepdims=True)
        p = jnp.sum(jnp.where(odd, jnp.where(lane == first, before, 0.0), here), axis=1, keepdims=True)
        v = jnp.sum(jnp.where(jnp.logical_and(odd, lane == first + 1), work[i], 0.0), axis=1, keepdims=True)
        m = q / p
        rows.append((work[i] - m * before) / jnp.sqrt(jnp.where(odd[:, :1], v - q * m, p)))
    return jnp.concatenate(rows, axis=0)[:, n:]


def inverse_of(zt):
    c = dot(zt, zt, ((1,), (1,)))
    n = c.shape[0]
    on = lax.broadcasted_iota(jnp.int32, (n, n), 0) == lax.broadcasted_iota(jnp.int32, (n, n), 1)
    diagonal = jnp.where(on, c, 0.0)
    down = 1.0 / jnp.sqrt(jnp.sum(diagonal, axis=1, keepdims=True))
    across = 1.0 / jnp.sqrt(jnp.sum(diagonal, axis=0, keepdims=True))
    return inverse_factor((c * down) * across) * across


def fold(stacked):
    return stacked[:64] + stacked[64:]


def split3(x):
    high = x.astype(BF16)
    rest = x - high.astype(F32)
    middle = rest.astype(BF16)
    return high, middle, (rest - middle.astype(F32)).astype(BF16)


def kernel(x_ref, start_ref, high, low, basis_ref, start_buf, buf, gram, triple, zacc, g3, zsend, zslots, zz, zall,
           start_sem, own_sem, send_sem, recv_sem, zsend_sem, rs_sem, zz_send_sem, zz_sem, ag_send_sem, ag_sem):
    w = lax.axis_index("wide")
    z = lax.axis_index("narrow")
    cc, xx, yy = lax.rem(w, CORES), lax.rem(w // CORES, NX), w // (CORES * NX)
    spectra, rows, cols = buf.shape[0], x_ref.shape[1], buf.shape[2]

    def peer(offset):
        y, x, c = offset
        return (lax.rem(yy + y, NY) * NX + lax.rem(xx + x, NX)) * CORES + lax.rem(cc + c, CORES)

    peers = [peer(offset) for offset in PEERS]
    far_first = [peer(offset) for offset in sorted(PEERS, key=lambda o: -min(o[0], NY - o[0]) - min(o[1], NX - o[1]))]
    depths = [lax.rem(z + d, NZ) for d in (2, 1, 3)]

    barrier = pltpu.get_barrier_semaphore()
    for t in far_first:
        pl.semaphore_signal(barrier, inc=1, device_id=(t, z), device_id_type=MESH)
    for d in depths:
        pl.semaphore_signal(barrier, inc=1, device_id=(w, d), device_id_type=MESH)
    my_rows = pl.ds(pl.multiple_of(w * rows, rows), rows)
    own = pltpu.make_async_copy(
        x_ref.at[:, :, pl.ds(pl.multiple_of(w * cols, cols), cols)], buf.at[:, my_rows, :], own_sem)
    own.start()
    begun = pltpu.make_async_copy(start_ref, start_buf, start_sem)
    begun.start()
    pl.semaphore_wait(barrier, len(peers) + len(depths))

    part = rows // PARTS

    def send(s):
        for r in range(PARTS):
            here = pl.ds(pl.multiple_of(w * rows + r * part, part), part)
            for t in peers:
                pltpu.make_async_remote_copy(
                    src_ref=x_ref.at[s, pl.ds(r * part, part), pl.ds(pl.multiple_of(t * cols, cols), cols)],
                    dst_ref=buf.at[s, here, :],
                    send_sem=send_sem, recv_sem=recv_sem.at[s], device_id=(t, z), device_id_type=MESH).start()

    def arrived(ref, sem):
        pltpu.make_async_copy(ref, ref, sem).wait()

    nt = ((1,), (1,))

    def multiply(s):
        arrived(buf.at[s, pl.ds(0, len(PEERS) * rows), :], recv_sem.at[s])
        h, l = split(buf[s])
        high[s] = h
        low[s] = l
        inner = dot(triple[...], h, exact=False) + dot(triple[...], l, exact=False)
        inner = jnp.concatenate(split(inner[:64] + (inner[64:128] + inner[128:])), axis=0)
        zacc[...] += fold(dot(inner, h, nt, False) + dot(inner, l, nt, False))

    def accumulate(s):
        h, l = high[s], low[s]
        gram[...] += (dot(h, h, nt, False) + dot(h, l, nt, False)) + (dot(l, h, nt, False) + dot(l, l, nt, False))

    @pl.loop(0, AHEAD)
    def _(s):
        send(s)

    gram[...] = jnp.zeros_like(gram)
    zacc[...] = jnp.zeros_like(zacc)
    begun.wait()
    start = start_buf[...]
    triple[...] = jnp.concatenate(split3(dot(inverse_of(start), start)), axis=0)
    own.wait()

    @pl.loop(0, spectra - AHEAD)
    def _(s):
        send(s + AHEAD)
        multiply(s)
        accumulate(s)

    @pl.loop(spectra - AHEAD, spectra - 1)
    def _(s):
        multiply(s)
        accumulate(s)

    multiply(spectra - 1)

    def tile(ref, t):
        return ref.at[pl.ds(pl.multiple_of(t // 4 * 8, 8), 8), pl.ds(pl.multiple_of(lax.rem(t, 4) * 128, 128), 128)]

    def reduce(it, value):
        zsend[it] = value
        for t in far_first:
            pltpu.make_async_remote_copy(
                src_ref=tile(zsend.at[it], t), dst_ref=zslots.at[it, w],
                send_sem=zsend_sem.at[it], recv_sem=rs_sem.at[it], device_id=(t, z), device_id_type=MESH).start()
        zslots[it, w] = tile(zsend.at[it], w)[...]

    def spread(it):
        arrived(zslots.at[it, pl.ds(0, len(PEERS))], rs_sem.at[it])
        zz[it, z] = jnp.sum(zslots[it], axis=0)
        for d in depths:
            pltpu.make_async_remote_copy(
                src_ref=zz.at[it, z], dst_ref=zz.at[it, z],
                send_sem=zz_send_sem.at[it], recv_sem=zz_sem.at[it], device_id=(w, d), device_id_type=MESH).start()
        arrived(zz.at[it, pl.ds(0, len(depths))], zz_sem.at[it])
        tile(zall.at[it], w)[...] = (zz[it, 0] + zz[it, 1]) + (zz[it, 2] + zz[it, 3])
        for t in far_first:
            pltpu.make_async_remote_copy(
                src_ref=tile(zall.at[it], w), dst_ref=tile(zall.at[it], w),
                send_sem=ag_send_sem.at[it], recv_sem=ag_sem.at[it], device_id=(t, z), device_id_type=MESH).start()

    def gathered(it):
        arrived(zslots.at[it, pl.ds(0, len(PEERS))], ag_sem.at[it])
        return zall[it]

    reduce(0, zacc[...])
    accumulate(spectra - 1)
    for i, g in enumerate(split3(gram[...])):
        g3[i] = g
    spread(0)
    z1 = gathered(0)
    zh, zm, zl = split3(z1)
    by_high = dot(jnp.concatenate([zh, zm, zl], axis=0), g3[0], exact=False)
    by_middle = dot(jnp.concatenate([zh, zm], axis=0), g3[1], exact=False)
    by_low = dot(zh, g3[2], exact=False)
    reduce(1, by_high[:64] + ((by_high[64:128] + by_middle[:64]) + ((by_high[128:] + by_middle[64:]) + by_low)))
    inv1 = inverse_of(z1)
    spread(1)
    z2 = dot(inv1, gathered(1))
    basis_ref[...] = dot(inverse_of(z2), z2)

    arrived(buf.at[:, pl.ds(0, len(PEERS) * rows), :], send_sem)
    for it in range(ITERS):
        arrived(zslots.at[it, pl.ds(0, len(PEERS))], zsend_sem.at[it])
        arrived(zz.at[it, pl.ds(0, len(depths))], zz_send_sem.at[it])
        arrived(zslots.at[it, pl.ds(0, len(PEERS))], ag_send_sem.at[it])


def project(high, low, basis_ref, core_ref, factor_ref):
    basis = basis_ref[...]
    bh, bl = split(basis)
    both = jnp.concatenate([bh, bl], axis=0)
    step = pl.program_id(0)

    @pl.when(step == 0)
    def _():
        factor_ref[...] = basis

    for i in range(core_ref.shape[0]):
        s = step * core_ref.shape[0] + i
        core_ref[i] = fold(dot(both, high[s], exact=False)) + dot(bh, low[s], exact=False)


def on_device(slab, start):
    spectra, rows, columns = slab.shape
    cols = columns // WIDE
    dma = pltpu.SemaphoreType.DMA
    vmem = pl.BlockSpec(memory_space=pltpu.VMEM)
    hbm = pl.BlockSpec(memory_space=pltpu.HBM)
    high, low, basis = pl.pallas_call(
        kernel,
        out_shape=(pltpu.VMEM((spectra, 512, cols), BF16), pltpu.VMEM((spectra, 512, cols), BF16),
                   pltpu.VMEM((64, 512), F32)),
        in_specs=[hbm, hbm],
        out_specs=(vmem, vmem, vmem),
        scratch_shapes=[
            pltpu.VMEM((64, 512), F32),
            pltpu.VMEM((spectra, 512, cols), F32),
            pltpu.VMEM((512, 512), F32),
            pltpu.VMEM((192, 512), BF16),
            pltpu.VMEM((64, 512), F32),
            pltpu.VMEM((3, 512, 512), BF16),
            pltpu.VMEM((ITERS, 64, 512), F32),
            pltpu.VMEM((ITERS, WIDE, 8, 128), F32),
            pltpu.VMEM((ITERS, NZ, 8, 128), F32),
            pltpu.VMEM((ITERS, 64, 512), F32),
            dma(()), dma(()), dma(()), dma((spectra,)),
            dma((ITERS,)), dma((ITERS,)), dma((ITERS,)), dma((ITERS,)), dma((ITERS,)), dma((ITERS,)),
        ],
        compiler_params=pltpu.CompilerParams(
            collective_id=0, has_side_effects=True, vmem_limit_bytes=KERNEL_VMEM),
    )(slab, start.T)
    core, factor_t = pl.pallas_call(
        project,
        grid=(spectra // GROUP,),
        out_shape=(jax.ShapeDtypeStruct((spectra, 64, cols), F32), jax.ShapeDtypeStruct((64, 512), F32)),
        in_specs=[vmem, vmem, vmem],
        out_specs=(pl.BlockSpec((GROUP, 64, cols), lambda g: (g, 0, 0)), pl.BlockSpec((64, 512), lambda g: (0, 0))),
        compiler_params=pltpu.CompilerParams(vmem_limit_bytes=PROJECT_VMEM),
    )(high, low, basis)
    return core, factor_t.T


def solution(mesh):
    return jax.shard_map(
        on_device,
        mesh=mesh,
        in_specs=(P("narrow", "wide", None), P()),
        out_specs=(P("narrow", None, "wide"), P()),
        check_vma=False,
    )
```

```python
import jax
import jax.numpy as jnp
from jax import lax
from jax.experimental import pallas as pl
from jax.experimental.pallas import tpu as pltpu
from jax.sharding import PartitionSpec as P

MESH = pl.DeviceIdType.MESH
F32, BF16 = jnp.float32, jnp.bfloat16
ITERS = 2
AHEAD = 8
PARTS = 2
GROUP = 8
KERNEL_VMEM = 52953088
PROJECT_VMEM = 8 * 2**20
NX, NY, CORES, NZ = 4, 4, 2, 4
WIDE = NX * NY * CORES
PEERS = [(y, x, c) for y in range(NY) for x in range(NX) for c in range(CORES) if (y, x, c) != (0, 0, 0)]

FAR_FIRST = sorted(PEERS, key=lambda o: -min(o[0], NY - o[0]) - min(o[1], NX - o[1]))
FAR_CHIPS = [o for o in FAR_FIRST if o[2] == 0]


def dot(a, b, dims=((1,), (0,)), exact=True):
    precision = lax.Precision.HIGHEST if exact else None
    return lax.dot_general(a, b, (dims, ((), ())), precision=precision, preferred_element_type=F32)


def split(x):
    high = x.astype(BF16)
    return high, (x - high.astype(F32)).astype(BF16)


def inverse_factor(gram2):
    n = gram2.shape[0]
    sub = lax.broadcasted_iota(jnp.int32, (8, 2 * n), 0)
    lane = lax.broadcasted_iota(jnp.int32, (8, 2 * n), 1)
    doubled = jnp.concatenate([gram2, gram2], axis=1)
    work = [jnp.where(lane < n, doubled[8 * i:8 * i + 8], (lane - n == sub + 8 * i).astype(F32)) for i in range(n // 8)]

    def spread(x):
        return jnp.broadcast_to(x, (8, 2 * n))

    for b in range(n // 8):
        k = 8 * b
        later = range(b + 1, n // 8)
        row = [spread(work[b][t:t + 1]) for t in range(8)]
        e = [[spread(work[b][t:t + 1, k + u:k + u + 1]) for u in range(t + 1)] for t in range(8)]
        column = {i: [spread(work[i][:, k + u:k + u + 1]) for u in range(8)] for i in later}
        update = {i: 0.0 for i in later}
        for p in range(0, 8, 2):
            aa, ab, bb = e[p][p], e[p + 1][p], e[p + 1][p + 1]
            inv = 1.0 / (aa * bb - ab * ab)
            y0 = (bb * row[p] - ab * row[p + 1]) * inv
            y1 = (aa * row[p + 1] - ab * row[p]) * inv
            f = {t: ((bb * e[t][p] - ab * e[t][p + 1]) * inv, (aa * e[t][p + 1] - ab * e[t][p]) * inv)
                 for t in range(p + 2, 8)}
            for i in later:
                update[i] = update[i] + (column[i][p] * y0 + column[i][p + 1] * y1)
                for t in range(p + 2, 8):
                    column[i][t] = column[i][t] - (column[i][p] * f[t][0] + column[i][p + 1] * f[t][1])
            for t in range(p + 2, 8):
                row[t] = row[t] - (e[t][p] * y0 + e[t][p + 1] * y1)
                for u in range(p + 2, t + 1):
                    e[t][u] = e[t][u] - (e[t][p] * f[u][0] + e[t][p + 1] * f[u][1])
        for t in range(2, 8):
            work[b] = jnp.where(sub == t, row[t], work[b])
        for i in later:
            work[i] = work[i] - update[i]

    odd = sub % 2 == 1
    rows = []
    for i in range(n // 8):
        first = sub - sub % 2 + 8 * i
        before = jnp.concatenate([work[i][7:8], work[i][:7]], axis=0)
        here = jnp.where(lane == first, work[i], 0.0)
        q = jnp.sum(jnp.where(odd, here, 0.0), axis=1, keepdims=True)
        p = jnp.sum(jnp.where(odd, jnp.where(lane == first, before, 0.0), here), axis=1, keepdims=True)
        v = jnp.sum(jnp.where(jnp.logical_and(odd, lane == first + 1), work[i], 0.0), axis=1, keepdims=True)
        m = q / p
        rows.append((work[i] - m * before) / jnp.sqrt(jnp.where(odd[:, :1], v - q * m, p)))
    return jnp.concatenate(rows, axis=0)[:, n:]


def inverse_of(zt):
    c = dot(zt, zt, ((1,), (1,)))
    n = c.shape[0]
    on = lax.broadcasted_iota(jnp.int32, (n, n), 0) == lax.broadcasted_iota(jnp.int32, (n, n), 1)
    diagonal = jnp.where(on, c, 0.0)
    down = 1.0 / jnp.sqrt(jnp.sum(diagonal, axis=1, keepdims=True))
    across = 1.0 / jnp.sqrt(jnp.sum(diagonal, axis=0, keepdims=True))
    return inverse_factor((c * down) * across) * across


def fold(stacked):
    return stacked[:64] + stacked[64:]


def split3(x):
    high = x.astype(BF16)
    rest = x - high.astype(F32)
    middle = rest.astype(BF16)
    return high, middle, (rest - middle.astype(F32)).astype(BF16)


def kernel(x_ref, start_ref, high, low, basis_ref, start_buf, buf, gram, triple, zacc, gram_rows, gram_other, gram_chip, gram_slots,
           zsend, zslots, zz, zall, wall,
           start_sem, own_sem, send_sem, recv_sem, zsend_sem, rs_sem, zz_send_sem, zz_sem, ag_send_sem, ag_sem,
           pair_send_sem, pair_sem, rows_send_sem, rows_sem):
    w = lax.axis_index("wide")
    z = lax.axis_index("narrow")
    cc, xx, yy = lax.rem(w, CORES), lax.rem(w // CORES, NX), w // (CORES * NX)
    spectra, rows, cols = buf.shape[0], x_ref.shape[1], buf.shape[2]

    def peer(offset):
        y, x, c = offset
        return (lax.rem(yy + y, NY) * NX + lax.rem(xx + x, NX)) * CORES + lax.rem(cc + c, CORES)

    peers = [peer(offset) for offset in PEERS]
    far_first = [peer(offset) for offset in FAR_FIRST]
    depths = [lax.rem(z + d, NZ) for d in (2, 1, 3)]

    barrier = pltpu.get_barrier_semaphore()
    for t in far_first:
        pl.semaphore_signal(barrier, inc=1, device_id=(t, z), device_id_type=MESH)
    for d in depths:
        pl.semaphore_signal(barrier, inc=1, device_id=(w, d), device_id_type=MESH)
    my_rows = pl.ds(pl.multiple_of(w * rows, rows), rows)
    own = pltpu.make_async_copy(
        x_ref.at[:, :, pl.ds(pl.multiple_of(w * cols, cols), cols)], buf.at[:, my_rows, :], own_sem)
    own.start()
    begun = pltpu.make_async_copy(start_ref, start_buf, start_sem)
    begun.start()
    pl.semaphore_wait(barrier, len(peers) + len(depths))

    part = rows // PARTS

    def send(s):
        for r in range(PARTS):
            here = pl.ds(pl.multiple_of(w * rows + r * part, part), part)
            for t in peers:
                pltpu.make_async_remote_copy(
                    src_ref=x_ref.at[s, pl.ds(r * part, part), pl.ds(pl.multiple_of(t * cols, cols), cols)],
                    dst_ref=buf.at[s, here, :],
                    send_sem=send_sem, recv_sem=recv_sem.at[s], device_id=(t, z), device_id_type=MESH).start()

    def arrived(ref, sem):
        pltpu.make_async_copy(ref, ref, sem).wait()

    nt = ((1,), (1,))

    def multiply(s):
        arrived(buf.at[s, pl.ds(0, len(PEERS) * rows), :], recv_sem.at[s])
        h, l = split(buf[s])
        high[s] = h
        low[s] = l
        inner = dot(triple[...], h, exact=False) + dot(triple[...], l, exact=False)
        inner = jnp.concatenate(split(inner[:64] + (inner[64:128] + inner[128:])), axis=0)
        zacc[...] += fold(dot(inner, h, nt, False) + dot(inner, l, nt, False))

    def accumulate(s):
        h, l = high[s], low[s]
        gram[...] += (dot(h, h, nt, False) + dot(h, l, nt, False)) + (dot(l, h, nt, False) + dot(l, l, nt, False))

    @pl.loop(0, AHEAD)
    def _(s):
        send(s)

    gram[...] = jnp.zeros_like(gram)
    zacc[...] = jnp.zeros_like(zacc)
    begun.wait()
    start = start_buf[...]
    triple[...] = jnp.concatenate(split3(dot(inverse_of(start), start)), axis=0)
    own.wait()

    @pl.loop(0, spectra - AHEAD)
    def _(s):
        send(s + AHEAD)
        multiply(s)
        accumulate(s)

    @pl.loop(spectra - AHEAD, spectra - 1)
    def _(s):
        multiply(s)
        accumulate(s)

    multiply(spectra - 1)

    def tile(ref, t):
        return ref.at[pl.ds(pl.multiple_of(t // 4 * 8, 8), 8), pl.ds(pl.multiple_of(lax.rem(t, 4) * 128, 128), 128)]

    def swap_planes(it, value):
        zz[it, z] = value
        for d in depths:
            pltpu.make_async_remote_copy(
                src_ref=zz.at[it, z], dst_ref=zz.at[it, z],
                send_sem=zz_send_sem.at[it], recv_sem=zz_sem.at[it], device_id=(w, d), device_id_type=MESH).start()

    def spread(it, place):
        arrived(zz.at[it, pl.ds(0, len(depths))], zz_sem.at[it])
        place[...] = (zz[it, 0] + zz[it, 1]) + (zz[it, 2] + zz[it, 3])
        for t in far_first:
            pltpu.make_async_remote_copy(
                src_ref=place, dst_ref=place,
                send_sem=ag_send_sem.at[it], recv_sem=ag_sem.at[it], device_id=(t, z), device_id_type=MESH).start()

    zsend[...] = zacc[...]
    for t in far_first:
        pltpu.make_async_remote_copy(
            src_ref=tile(zsend, t), dst_ref=zslots.at[w],
            send_sem=zsend_sem, recv_sem=rs_sem, device_id=(t, z), device_id_type=MESH).start()
    zslots[w] = tile(zsend, w)[...]

    accumulate(spectra - 1)
    gram_rows[...] = gram[...].reshape(gram_rows.shape)
    other = peer((0, 0, 1))
    pltpu.make_async_remote_copy(
        src_ref=gram_rows.at[:, :, 1 - cc], dst_ref=gram_other,
        send_sem=pair_send_sem, recv_sem=pair_sem, device_id=(other, z), device_id_type=MESH).start()
    arrived(gram_other, pair_sem)
    gram_chip[...] = gram_rows[:, :, cc] + gram_other[...]
    chip = w // CORES
    for offset in FAR_CHIPS:
        t = peer(offset)
        pltpu.make_async_remote_copy(
            src_ref=gram_chip.at[:, t // CORES], dst_ref=gram_slots.at[chip],
            send_sem=rows_send_sem, recv_sem=rows_sem, device_id=(t, z), device_id_type=MESH).start()
    gram_slots[chip] = gram_chip[:, chip]

    arrived(zslots.at[pl.ds(0, len(PEERS))], rs_sem)
    swap_planes(0, jnp.sum(zslots[...], axis=0))
    spread(0, tile(zall, w))
    arrived(zslots.at[pl.ds(0, len(PEERS))], ag_sem.at[0])
    z1 = zall[...]

    arrived(gram_slots.at[pl.ds(0, len(FAR_CHIPS))], rows_sem)
    mine = dot(jnp.sum(gram_slots[...], axis=0).reshape(16, 512), z1, nt)
    swap_planes(1, jnp.concatenate([mine[:8], mine[8:]], axis=1))
    inv1 = inverse_of(z1)
    spread(1, wall.at[pl.ds(pl.multiple_of(w * 8, 8), 8), :])
    arrived(zslots.at[pl.ds(0, len(PEERS))], ag_sem.at[1])
    z2 = jnp.concatenate([dot(inv1, wall[:, :64], nt), dot(inv1, wall[:, 64:], nt)], axis=1)
    basis_ref[...] = dot(inverse_of(z2), z2)

    arrived(buf.at[:, pl.ds(0, len(PEERS) * rows), :], send_sem)
    arrived(zslots.at[pl.ds(0, len(PEERS))], zsend_sem)
    arrived(gram_other, pair_send_sem)
    arrived(gram_slots.at[pl.ds(0, len(FAR_CHIPS))], rows_send_sem)
    for it in range(ITERS):
        arrived(zz.at[it, pl.ds(0, len(depths))], zz_send_sem.at[it])
        arrived(zslots.at[pl.ds(0, len(PEERS))], ag_send_sem.at[it])


def project(high, low, basis_ref, core_ref, factor_ref):
    basis = basis_ref[...]
    bh, bl = split(basis)
    both = jnp.concatenate([bh, bl], axis=0)
    step = pl.program_id(0)

    @pl.when(step == 0)
    def _():
        factor_ref[...] = basis

    for i in range(core_ref.shape[0]):
        s = step * core_ref.shape[0] + i
        core_ref[i] = fold(dot(both, high[s], exact=False)) + dot(bh, low[s], exact=False)


def on_device(slab, start):
    spectra, rows, columns = slab.shape
    cols = columns // WIDE
    dma = pltpu.SemaphoreType.DMA
    vmem = pl.BlockSpec(memory_space=pltpu.VMEM)
    hbm = pl.BlockSpec(memory_space=pltpu.HBM)
    high, low, basis = pl.pallas_call(
        kernel,
        out_shape=(pltpu.VMEM((spectra, 512, cols), BF16), pltpu.VMEM((spectra, 512, cols), BF16),
                   pltpu.VMEM((64, 512), F32)),
        in_specs=[hbm, hbm],
        out_specs=(vmem, vmem, vmem),
        scratch_shapes=[
            pltpu.VMEM((64, 512), F32),
            pltpu.VMEM((spectra, 512, cols), F32),
            pltpu.VMEM((512, 512), F32),
            pltpu.VMEM((192, 512), BF16),
            pltpu.VMEM((64, 512), F32),
            pltpu.VMEM((2, WIDE // CORES, CORES, 8, 512), F32),
            pltpu.VMEM((2, WIDE // CORES, 8, 512), F32),
            pltpu.VMEM((2, WIDE // CORES, 8, 512), F32),
            pltpu.VMEM((WIDE // CORES, 2, 8, 512), F32),
            pltpu.VMEM((64, 512), F32),
            pltpu.VMEM((WIDE, 8, 128), F32),
            pltpu.VMEM((ITERS, NZ, 8, 128), F32),
            pltpu.VMEM((64, 512), F32),
            pltpu.VMEM((256, 128), F32),
            dma(()), dma(()), dma(()), dma((spectra,)),
            dma(()), dma(()), dma((ITERS,)), dma((ITERS,)), dma((ITERS,)), dma((ITERS,)),
            dma(()), dma(()), dma(()), dma(()),
        ],
        compiler_params=pltpu.CompilerParams(
            collective_id=0, has_side_effects=True, vmem_limit_bytes=KERNEL_VMEM),
    )(slab, start.T)
    core, factor_t = pl.pallas_call(
        project,
        grid=(spectra // GROUP,),
        out_shape=(jax.ShapeDtypeStruct((spectra, 64, cols), F32), jax.ShapeDtypeStruct((64, 512), F32)),
        in_specs=[vmem, vmem, vmem],
        out_specs=(pl.BlockSpec((GROUP, 64, cols), lambda g: (g, 0, 0)), pl.BlockSpec((64, 512), lambda g: (0, 0))),
        compiler_params=pltpu.CompilerParams(vmem_limit_bytes=PROJECT_VMEM),
    )(high, low, basis)
    return core, factor_t.T


def solution(mesh):
    return jax.shard_map(
        on_device,
        mesh=mesh,
        in_specs=(P("narrow", "wide", None), P()),
        out_specs=(P("narrow", None, "wide"), P()),
        check_vma=False,
    )
```

```python
import jax
import jax.numpy as jnp
from jax import lax
from jax.experimental import pallas as pl
from jax.experimental.pallas import tpu as pltpu
from jax.sharding import PartitionSpec as P

MESH = pl.DeviceIdType.MESH
F32, BF16 = jnp.float32, jnp.bfloat16
ITERS = 2
AHEAD = 8
PARTS = 2
GROUP = 8
KERNEL_VMEM = 52953088
PROJECT_VMEM = 8 * 2**20
NX, NY, CORES, NZ = 4, 4, 2, 4
WIDE = NX * NY * CORES
PEERS = [(y, x, c) for y in range(NY) for x in range(NX) for c in range(CORES) if (y, x, c) != (0, 0, 0)]

FAR_FIRST = sorted(PEERS, key=lambda o: -min(o[0], NY - o[0]) - min(o[1], NX - o[1]))
FAR_CHIPS = [o for o in FAR_FIRST if o[2] == 0]


def dot(a, b, dims=((1,), (0,)), exact=True):
    precision = lax.Precision.HIGHEST if exact else None
    return lax.dot_general(a, b, (dims, ((), ())), precision=precision, preferred_element_type=F32)


def split(x):
    high = x.astype(BF16)
    return high, (x - high.astype(F32)).astype(BF16)


def inverse_factor(gram2):
    n = gram2.shape[0]
    sub = lax.broadcasted_iota(jnp.int32, (8, 2 * n), 0)
    lane = lax.broadcasted_iota(jnp.int32, (8, 2 * n), 1)
    doubled = jnp.concatenate([gram2, gram2], axis=1)
    work = [jnp.where(lane < n, doubled[8 * i:8 * i + 8], (lane - n == sub + 8 * i).astype(F32)) for i in range(n // 8)]

    def spread(x):
        return jnp.broadcast_to(x, (8, 2 * n))

    for b in range(n // 8):
        k = 8 * b
        later = range(b + 1, n // 8)
        row = [spread(work[b][t:t + 1]) for t in range(8)]
        e = [[spread(work[b][t:t + 1, k + u:k + u + 1]) for u in range(t + 1)] for t in range(8)]
        column = {i: [spread(work[i][:, k + u:k + u + 1]) for u in range(8)] for i in later}
        update = {i: 0.0 for i in later}
        for p in range(0, 8, 2):
            aa, ab, bb = e[p][p], e[p + 1][p], e[p + 1][p + 1]
            inv = 1.0 / (aa * bb - ab * ab)
            y0 = (bb * row[p] - ab * row[p + 1]) * inv
            y1 = (aa * row[p + 1] - ab * row[p]) * inv
            f = {t: ((bb * e[t][p] - ab * e[t][p + 1]) * inv, (aa * e[t][p + 1] - ab * e[t][p]) * inv)
                 for t in range(p + 2, 8)}
            for i in later:
                update[i] = update[i] + (column[i][p] * y0 + column[i][p + 1] * y1)
                for t in range(p + 2, 8):
                    column[i][t] = column[i][t] - (column[i][p] * f[t][0] + column[i][p + 1] * f[t][1])
            for t in range(p + 2, 8):
                row[t] = row[t] - (e[t][p] * y0 + e[t][p + 1] * y1)
                for u in range(p + 2, t + 1):
                    e[t][u] = e[t][u] - (e[t][p] * f[u][0] + e[t][p + 1] * f[u][1])
        for t in range(2, 8):
            work[b] = jnp.where(sub == t, row[t], work[b])
        for i in later:
            work[i] = work[i] - update[i]

    odd = sub % 2 == 1
    rows = []
    for i in range(n // 8):
        first = sub - sub % 2 + 8 * i
        before = jnp.concatenate([work[i][7:8], work[i][:7]], axis=0)
        here = jnp.where(lane == first, work[i], 0.0)
        q = jnp.sum(jnp.where(odd, here, 0.0), axis=1, keepdims=True)
        p = jnp.sum(jnp.where(odd, jnp.where(lane == first, before, 0.0), here), axis=1, keepdims=True)
        v = jnp.sum(jnp.where(jnp.logical_and(odd, lane == first + 1), work[i], 0.0), axis=1, keepdims=True)
        m = q / p
        rows.append((work[i] - m * before) / jnp.sqrt(jnp.where(odd[:, :1], v - q * m, p)))
    return jnp.concatenate(rows, axis=0)[:, n:]


def inverse_of(zt):
    c = dot(zt, zt, ((1,), (1,)))
    n = c.shape[0]
    on = lax.broadcasted_iota(jnp.int32, (n, n), 0) == lax.broadcasted_iota(jnp.int32, (n, n), 1)
    diagonal = jnp.where(on, c, 0.0)
    down = 1.0 / jnp.sqrt(jnp.sum(diagonal, axis=1, keepdims=True))
    across = 1.0 / jnp.sqrt(jnp.sum(diagonal, axis=0, keepdims=True))
    return inverse_factor((c * down) * across) * across


def fold(stacked):
    return stacked[:64] + stacked[64:]


def split3(x):
    high = x.astype(BF16)
    rest = x - high.astype(F32)
    middle = rest.astype(BF16)
    return high, middle, (rest - middle.astype(F32)).astype(BF16)


def kernel(x_ref, start_ref, high, low, basis_ref, start_buf, buf, gram, triple, zacc, gram_rows, gram_other, gram_chip, gram_slots, gram_planes,
           zsend, zslots, zz, zall, wall,
           start_sem, own_sem, send_sem, recv_sem, zsend_sem, rs_sem, zz_send_sem, zz_sem, ag_send_sem, ag_sem,
           pair_send_sem, pair_sem, rows_send_sem, rows_sem, planes_send_sem, planes_sem):
    w = lax.axis_index("wide")
    z = lax.axis_index("narrow")
    cc, xx, yy = lax.rem(w, CORES), lax.rem(w // CORES, NX), w // (CORES * NX)
    spectra, rows, cols = buf.shape[0], x_ref.shape[1], buf.shape[2]

    def peer(offset):
        y, x, c = offset
        return (lax.rem(yy + y, NY) * NX + lax.rem(xx + x, NX)) * CORES + lax.rem(cc + c, CORES)

    peers = [peer(offset) for offset in PEERS]
    far_first = [peer(offset) for offset in FAR_FIRST]
    depths = [lax.rem(z + d, NZ) for d in (2, 1, 3)]

    barrier = pltpu.get_barrier_semaphore()
    for t in far_first:
        pl.semaphore_signal(barrier, inc=1, device_id=(t, z), device_id_type=MESH)
    for d in depths:
        pl.semaphore_signal(barrier, inc=1, device_id=(w, d), device_id_type=MESH)
    my_rows = pl.ds(pl.multiple_of(w * rows, rows), rows)
    own = pltpu.make_async_copy(
        x_ref.at[:, :, pl.ds(pl.multiple_of(w * cols, cols), cols)], buf.at[:, my_rows, :], own_sem)
    own.start()
    begun = pltpu.make_async_copy(start_ref, start_buf, start_sem)
    begun.start()
    pl.semaphore_wait(barrier, len(peers) + len(depths))

    part = rows // PARTS

    def send(s):
        for r in range(PARTS):
            here = pl.ds(pl.multiple_of(w * rows + r * part, part), part)
            for t in peers:
                pltpu.make_async_remote_copy(
                    src_ref=x_ref.at[s, pl.ds(r * part, part), pl.ds(pl.multiple_of(t * cols, cols), cols)],
                    dst_ref=buf.at[s, here, :],
                    send_sem=send_sem, recv_sem=recv_sem.at[s], device_id=(t, z), device_id_type=MESH).start()

    def arrived(ref, sem):
        pltpu.make_async_copy(ref, ref, sem).wait()

    nt = ((1,), (1,))

    def multiply(s):
        arrived(buf.at[s, pl.ds(0, len(PEERS) * rows), :], recv_sem.at[s])
        h, l = split(buf[s])
        high[s] = h
        low[s] = l
        inner = dot(triple[...], h, exact=False) + dot(triple[...], l, exact=False)
        inner = jnp.concatenate(split(inner[:64] + (inner[64:128] + inner[128:])), axis=0)
        zacc[...] += fold(dot(inner, h, nt, False) + dot(inner, l, nt, False))

    def accumulate(s):
        h, l = high[s], low[s]
        gram[...] += (dot(h, h, nt, False) + dot(h, l, nt, False)) + (dot(l, h, nt, False) + dot(l, l, nt, False))

    @pl.loop(0, AHEAD)
    def _(s):
        send(s)

    gram[...] = jnp.zeros_like(gram)
    zacc[...] = jnp.zeros_like(zacc)
    begun.wait()
    start = start_buf[...]
    triple[...] = jnp.concatenate(split3(dot(inverse_of(start), start)), axis=0)
    own.wait()

    @pl.loop(0, spectra - AHEAD)
    def _(s):
        send(s + AHEAD)
        multiply(s)
        accumulate(s)

    @pl.loop(spectra - AHEAD, spectra - 1)
    def _(s):
        multiply(s)
        accumulate(s)

    multiply(spectra - 1)

    def tile(ref, t):
        return ref.at[pl.ds(pl.multiple_of(t // 4 * 8, 8), 8), pl.ds(pl.multiple_of(lax.rem(t, 4) * 128, 128), 128)]

    def swap_planes(ref, sends, sem):
        for d in depths:
            pltpu.make_async_remote_copy(
                src_ref=ref.at[z], dst_ref=ref.at[z],
                send_sem=sends, recv_sem=sem, device_id=(w, d), device_id_type=MESH).start()

    def four_planes(ref, sem):
        arrived(ref.at[pl.ds(0, len(depths))], sem)
        return (ref[0] + ref[1]) + (ref[2] + ref[3])

    def spread(it, place, value):
        place[...] = value
        for t in far_first:
            pltpu.make_async_remote_copy(
                src_ref=place, dst_ref=place,
                send_sem=ag_send_sem.at[it], recv_sem=ag_sem.at[it], device_id=(t, z), device_id_type=MESH).start()

    zsend[...] = zacc[...]
    for t in far_first:
        pltpu.make_async_remote_copy(
            src_ref=tile(zsend, t), dst_ref=zslots.at[w],
            send_sem=zsend_sem, recv_sem=rs_sem, device_id=(t, z), device_id_type=MESH).start()
    zslots[w] = tile(zsend, w)[...]

    accumulate(spectra - 1)
    gram_rows[...] = gram[...].reshape(gram_rows.shape)
    other = peer((0, 0, 1))
    pltpu.make_async_remote_copy(
        src_ref=gram_rows.at[:, :, 1 - cc], dst_ref=gram_other,
        send_sem=pair_send_sem, recv_sem=pair_sem, device_id=(other, z), device_id_type=MESH).start()
    arrived(gram_other, pair_sem)
    gram_chip[...] = gram_rows[:, :, cc] + gram_other[...]
    chip = w // CORES
    for offset in FAR_CHIPS:
        t = peer(offset)
        pltpu.make_async_remote_copy(
            src_ref=gram_chip.at[:, t // CORES], dst_ref=gram_slots.at[chip],
            send_sem=rows_send_sem, recv_sem=rows_sem, device_id=(t, z), device_id_type=MESH).start()
    gram_slots[chip] = gram_chip[:, chip]

    arrived(zslots.at[pl.ds(0, len(PEERS))], rs_sem)
    zz[z] = jnp.sum(zslots[...], axis=0)
    swap_planes(zz, zz_send_sem, zz_sem)
    spread(0, tile(zall, w), four_planes(zz, zz_sem))

    arrived(gram_slots.at[pl.ds(0, len(FAR_CHIPS))], rows_sem)
    gram_planes[z] = jnp.sum(gram_slots[...], axis=0)
    swap_planes(gram_planes, planes_send_sem, planes_sem)

    arrived(zslots.at[pl.ds(0, len(PEERS))], ag_sem.at[0])
    z1 = zall[...]

    b1 = dot(inverse_of(z1), z1)
    mine = dot(four_planes(gram_planes, planes_sem).reshape(16, 512), b1, nt)
    spread(1, wall.at[pl.ds(pl.multiple_of(w * 8, 8), 8), :], jnp.concatenate([mine[:8], mine[8:]], axis=1))
    arrived(zslots.at[pl.ds(0, len(PEERS))], ag_sem.at[1])
    halves = wall[...].T
    z2 = jnp.concatenate([halves[:64], halves[64:]], axis=1)
    basis_ref[...] = dot(inverse_of(z2), z2)

    arrived(buf.at[:, pl.ds(0, len(PEERS) * rows), :], send_sem)
    arrived(zslots.at[pl.ds(0, len(PEERS))], zsend_sem)
    arrived(gram_other, pair_send_sem)
    arrived(gram_slots.at[pl.ds(0, len(FAR_CHIPS))], rows_send_sem)
    arrived(zz.at[pl.ds(0, len(depths))], zz_send_sem)
    arrived(gram_planes.at[pl.ds(0, len(depths))], planes_send_sem)
    for it in range(ITERS):
        arrived(zslots.at[pl.ds(0, len(PEERS))], ag_send_sem.at[it])


def project(high, low, basis_ref, core_ref, factor_ref):
    basis = basis_ref[...]
    bh, bl = split(basis)
    both = jnp.concatenate([bh, bl], axis=0)
    step = pl.program_id(0)

    @pl.when(step == 0)
    def _():
        factor_ref[...] = basis

    for i in range(core_ref.shape[0]):
        s = step * core_ref.shape[0] + i
        core_ref[i] = fold(dot(both, high[s], exact=False)) + dot(bh, low[s], exact=False)


def on_device(slab, start):
    spectra, rows, columns = slab.shape
    cols = columns // WIDE
    dma = pltpu.SemaphoreType.DMA
    vmem = pl.BlockSpec(memory_space=pltpu.VMEM)
    hbm = pl.BlockSpec(memory_space=pltpu.HBM)
    high, low, basis = pl.pallas_call(
        kernel,
        out_shape=(pltpu.VMEM((spectra, 512, cols), BF16), pltpu.VMEM((spectra, 512, cols), BF16),
                   pltpu.VMEM((64, 512), F32)),
        in_specs=[hbm, hbm],
        out_specs=(vmem, vmem, vmem),
        scratch_shapes=[
            pltpu.VMEM((64, 512), F32),
            pltpu.VMEM((spectra, 512, cols), F32),
            pltpu.VMEM((512, 512), F32),
            pltpu.VMEM((192, 512), BF16),
            pltpu.VMEM((64, 512), F32),
            pltpu.VMEM((2, WIDE // CORES, CORES, 8, 512), F32),
            pltpu.VMEM((2, WIDE // CORES, 8, 512), F32),
            pltpu.VMEM((2, WIDE // CORES, 8, 512), F32),
            pltpu.VMEM((WIDE // CORES, 2, 8, 512), F32),
            pltpu.VMEM((NZ, 2, 8, 512), F32),
            pltpu.VMEM((64, 512), F32),
            pltpu.VMEM((WIDE, 8, 128), F32),
            pltpu.VMEM((NZ, 8, 128), F32),
            pltpu.VMEM((64, 512), F32),
            pltpu.VMEM((256, 128), F32),
            dma(()), dma(()), dma(()), dma((spectra,)),
            dma(()), dma(()), dma(()), dma(()), dma((ITERS,)), dma((ITERS,)),
            dma(()), dma(()), dma(()), dma(()), dma(()), dma(()),
        ],
        compiler_params=pltpu.CompilerParams(
            collective_id=0, has_side_effects=True, vmem_limit_bytes=KERNEL_VMEM),
    )(slab, start.T)
    core, factor_t = pl.pallas_call(
        project,
        grid=(spectra // GROUP,),
        out_shape=(jax.ShapeDtypeStruct((spectra, 64, cols), F32), jax.ShapeDtypeStruct((64, 512), F32)),
        in_specs=[vmem, vmem, vmem],
        out_specs=(pl.BlockSpec((GROUP, 64, cols), lambda g: (g, 0, 0)), pl.BlockSpec((64, 512), lambda g: (0, 0))),
        compiler_params=pltpu.CompilerParams(vmem_limit_bytes=PROJECT_VMEM),
    )(high, low, basis)
    return core, factor_t.T


def solution(mesh):
    return jax.shard_map(
        on_device,
        mesh=mesh,
        in_specs=(P("narrow", "wide", None), P()),
        out_specs=(P("narrow", None, "wide"), P()),
        check_vma=False,
    )
```

```python
import jax
import jax.numpy as jnp
from jax import lax
from jax.experimental import pallas as pl
from jax.experimental.pallas import tpu as pltpu
from jax.sharding import PartitionSpec as P

MESH = pl.DeviceIdType.MESH
F32, BF16 = jnp.float32, jnp.bfloat16
ITERS = 2
AHEAD = 8
PARTS = 1
GROUP = 8
KERNEL_VMEM = 52953088
PROJECT_VMEM = 8 * 2**20
NX, NY, CORES, NZ = 4, 4, 2, 4
WIDE = NX * NY * CORES
PEERS = [(y, x, c) for y in range(NY) for x in range(NX) for c in range(CORES) if (y, x, c) != (0, 0, 0)]

FAR_FIRST = sorted(PEERS, key=lambda o: -min(o[0], NY - o[0]) - min(o[1], NX - o[1]))
FAR_CHIPS = [o for o in FAR_FIRST if o[2] == 0]


def dot(a, b, dims=((1,), (0,)), exact=True):
    precision = lax.Precision.HIGHEST if exact else None
    return lax.dot_general(a, b, (dims, ((), ())), precision=precision, preferred_element_type=F32)


def split(x):
    high = x.astype(BF16)
    return high, (x - high.astype(F32)).astype(BF16)


def inverse_factor(gram2):
    n = gram2.shape[0]
    sub = lax.broadcasted_iota(jnp.int32, (8, 2 * n), 0)
    lane = lax.broadcasted_iota(jnp.int32, (8, 2 * n), 1)
    doubled = jnp.concatenate([gram2, gram2], axis=1)
    work = [jnp.where(lane < n, doubled[8 * i:8 * i + 8], (lane - n == sub + 8 * i).astype(F32)) for i in range(n // 8)]

    def spread(x):
        return jnp.broadcast_to(x, (8, 2 * n))

    for b in range(n // 8):
        k = 8 * b
        later = range(b + 1, n // 8)
        row = [spread(work[b][t:t + 1]) for t in range(8)]
        e = [[spread(work[b][t:t + 1, k + u:k + u + 1]) for u in range(t + 1)] for t in range(8)]
        column = {i: [spread(work[i][:, k + u:k + u + 1]) for u in range(8)] for i in later}
        update = {i: 0.0 for i in later}
        for p in range(0, 8, 2):
            aa, ab, bb = e[p][p], e[p + 1][p], e[p + 1][p + 1]
            inv = 1.0 / (aa * bb - ab * ab)
            y0 = (bb * row[p] - ab * row[p + 1]) * inv
            y1 = (aa * row[p + 1] - ab * row[p]) * inv
            f = {t: ((bb * e[t][p] - ab * e[t][p + 1]) * inv, (aa * e[t][p + 1] - ab * e[t][p]) * inv)
                 for t in range(p + 2, 8)}
            for i in later:
                update[i] = update[i] + (column[i][p] * y0 + column[i][p + 1] * y1)
                for t in range(p + 2, 8):
                    column[i][t] = column[i][t] - (column[i][p] * f[t][0] + column[i][p + 1] * f[t][1])
            for t in range(p + 2, 8):
                row[t] = row[t] - (e[t][p] * y0 + e[t][p + 1] * y1)
                for u in range(p + 2, t + 1):
                    e[t][u] = e[t][u] - (e[t][p] * f[u][0] + e[t][p + 1] * f[u][1])
        for t in range(2, 8):
            work[b] = jnp.where(sub == t, row[t], work[b])
        for i in later:
            work[i] = work[i] - update[i]

    odd = sub % 2 == 1
    rows = []
    for i in range(n // 8):
        first = sub - sub % 2 + 8 * i
        before = jnp.concatenate([work[i][7:8], work[i][:7]], axis=0)
        here = jnp.where(lane == first, work[i], 0.0)
        q = jnp.sum(jnp.where(odd, here, 0.0), axis=1, keepdims=True)
        p = jnp.sum(jnp.where(odd, jnp.where(lane == first, before, 0.0), here), axis=1, keepdims=True)
        v = jnp.sum(jnp.where(jnp.logical_and(odd, lane == first + 1), work[i], 0.0), axis=1, keepdims=True)
        m = q / p
        rows.append((work[i] - m * before) / jnp.sqrt(jnp.where(odd[:, :1], v - q * m, p)))
    return jnp.concatenate(rows, axis=0)[:, n:]


def inverse_of(zt):
    c = dot(zt, zt, ((1,), (1,)))
    n = c.shape[0]
    on = lax.broadcasted_iota(jnp.int32, (n, n), 0) == lax.broadcasted_iota(jnp.int32, (n, n), 1)
    diagonal = jnp.where(on, c, 0.0)
    down = 1.0 / jnp.sqrt(jnp.sum(diagonal, axis=1, keepdims=True))
    across = 1.0 / jnp.sqrt(jnp.sum(diagonal, axis=0, keepdims=True))
    return inverse_factor((c * down) * across) * across


def fold(stacked):
    return stacked[:64] + stacked[64:]


def split3(x):
    high = x.astype(BF16)
    rest = x - high.astype(F32)
    middle = rest.astype(BF16)
    return high, middle, (rest - middle.astype(F32)).astype(BF16)


def kernel(x_ref, start_ref, high, low, basis_ref, start_buf, buf, gram, triple, zacc, gram_rows, gram_other, gram_chip, gram_slots, gram_planes,
           zsend, zslots, zz, zall, wall,
           start_sem, own_sem, send_sem, recv_sem, zsend_sem, rs_sem, zz_send_sem, zz_sem, ag_send_sem, ag_sem,
           pair_send_sem, pair_sem, rows_send_sem, rows_sem, planes_send_sem, planes_sem):
    w = lax.axis_index("wide")
    z = lax.axis_index("narrow")
    cc, xx, yy = lax.rem(w, CORES), lax.rem(w // CORES, NX), w // (CORES * NX)
    spectra, rows, cols = buf.shape[0], x_ref.shape[1], buf.shape[2]

    def peer(offset):
        y, x, c = offset
        return (lax.rem(yy + y, NY) * NX + lax.rem(xx + x, NX)) * CORES + lax.rem(cc + c, CORES)

    peers = [peer(offset) for offset in PEERS]
    far_first = [peer(offset) for offset in FAR_FIRST]
    depths = [lax.rem(z + d, NZ) for d in (2, 1, 3)]

    barrier = pltpu.get_barrier_semaphore()
    for t in far_first:
        pl.semaphore_signal(barrier, inc=1, device_id=(t, z), device_id_type=MESH)
    for d in depths:
        pl.semaphore_signal(barrier, inc=1, device_id=(w, d), device_id_type=MESH)
    my_rows = pl.ds(pl.multiple_of(w * rows, rows), rows)
    own = pltpu.make_async_copy(
        x_ref.at[:, :, pl.ds(pl.multiple_of(w * cols, cols), cols)], buf.at[:, my_rows, :], own_sem)
    own.start()
    begun = pltpu.make_async_copy(start_ref, start_buf, start_sem)
    begun.start()
    pl.semaphore_wait(barrier, len(peers) + len(depths))

    part = rows // PARTS

    def send(s):
        for r in range(PARTS):
            here = pl.ds(pl.multiple_of(w * rows + r * part, part), part)
            for t in far_first:
                pltpu.make_async_remote_copy(
                    src_ref=x_ref.at[s, pl.ds(r * part, part), pl.ds(pl.multiple_of(t * cols, cols), cols)],
                    dst_ref=buf.at[s, here, :],
                    send_sem=send_sem, recv_sem=recv_sem.at[s], device_id=(t, z), device_id_type=MESH).start()

    def arrived(ref, sem):
        pltpu.make_async_copy(ref, ref, sem).wait()

    nt = ((1,), (1,))

    def multiply(s):
        arrived(buf.at[s, pl.ds(0, len(PEERS) * rows), :], recv_sem.at[s])
        h, l = split(buf[s])
        high[s] = h
        low[s] = l
        inner = dot(triple[...], h, exact=False) + dot(triple[...], l, exact=False)
        inner = jnp.concatenate(split(inner[:64] + (inner[64:128] + inner[128:])), axis=0)
        zacc[...] += fold(dot(inner, h, nt, False) + dot(inner, l, nt, False))

    def accumulate(s):
        h, l = high[s], low[s]
        gram[...] += (dot(h, h, nt, False) + dot(h, l, nt, False)) + (dot(l, h, nt, False) + dot(l, l, nt, False))

    @pl.loop(0, AHEAD)
    def _(s):
        send(s)

    gram[...] = jnp.zeros_like(gram)
    zacc[...] = jnp.zeros_like(zacc)
    begun.wait()
    start = start_buf[...]
    triple[...] = jnp.concatenate(split3(dot(inverse_of(start), start)), axis=0)
    own.wait()

    @pl.loop(0, spectra - AHEAD)
    def _(s):
        send(s + AHEAD)
        multiply(s)
        accumulate(s)

    @pl.loop(spectra - AHEAD, spectra - 1)
    def _(s):
        multiply(s)
        accumulate(s)

    multiply(spectra - 1)

    def tile(ref, t):
        return ref.at[pl.ds(pl.multiple_of(t // 4 * 8, 8), 8), pl.ds(pl.multiple_of(lax.rem(t, 4) * 128, 128), 128)]

    def swap_planes(ref, sends, sem):
        for d in depths:
            pltpu.make_async_remote_copy(
                src_ref=ref.at[z], dst_ref=ref.at[z],
                send_sem=sends, recv_sem=sem, device_id=(w, d), device_id_type=MESH).start()

    def four_planes(ref, sem):
        arrived(ref.at[pl.ds(0, len(depths))], sem)
        return (ref[0] + ref[1]) + (ref[2] + ref[3])

    def spread(it, place, value):
        place[...] = value
        for t in far_first:
            pltpu.make_async_remote_copy(
                src_ref=place, dst_ref=place,
                send_sem=ag_send_sem.at[it], recv_sem=ag_sem.at[it], device_id=(t, z), device_id_type=MESH).start()

    zsend[...] = zacc[...]
    for t in far_first:
        pltpu.make_async_remote_copy(
            src_ref=tile(zsend, t), dst_ref=zslots.at[w],
            send_sem=zsend_sem, recv_sem=rs_sem, device_id=(t, z), device_id_type=MESH).start()
    zslots[w] = tile(zsend, w)[...]

    accumulate(spectra - 1)
    gram_rows[...] = gram[...].reshape(gram_rows.shape)
    other = peer((0, 0, 1))
    pltpu.make_async_remote_copy(
        src_ref=gram_rows.at[:, :, 1 - cc], dst_ref=gram_other,
        send_sem=pair_send_sem, recv_sem=pair_sem, device_id=(other, z), device_id_type=MESH).start()
    arrived(gram_other, pair_sem)
    gram_chip[...] = gram_rows[:, :, cc] + gram_other[...]
    chip = w // CORES
    for offset in FAR_CHIPS:
        t = peer(offset)
        pltpu.make_async_remote_copy(
            src_ref=gram_chip.at[:, t // CORES], dst_ref=gram_slots.at[chip],
            send_sem=rows_send_sem, recv_sem=rows_sem, device_id=(t, z), device_id_type=MESH).start()
    gram_slots[chip] = gram_chip[:, chip]

    arrived(zslots.at[pl.ds(0, len(PEERS))], rs_sem)
    zz[z] = jnp.sum(zslots[...], axis=0)
    swap_planes(zz, zz_send_sem, zz_sem)
    spread(0, tile(zall, w), four_planes(zz, zz_sem))

    arrived(gram_slots.at[pl.ds(0, len(FAR_CHIPS))], rows_sem)
    gram_planes[z] = jnp.sum(gram_slots[...], axis=0)
    swap_planes(gram_planes, planes_send_sem, planes_sem)

    arrived(zslots.at[pl.ds(0, len(PEERS))], ag_sem.at[0])
    z1 = zall[...]

    b1 = dot(inverse_of(z1), z1)
    mine = dot(four_planes(gram_planes, planes_sem).reshape(16, 512), b1, nt)
    spread(1, wall.at[pl.ds(pl.multiple_of(w * 8, 8), 8), :], jnp.concatenate([mine[:8], mine[8:]], axis=1))
    arrived(zslots.at[pl.ds(0, len(PEERS))], ag_sem.at[1])
    halves = wall[...].T
    z2 = jnp.concatenate([halves[:64], halves[64:]], axis=1)
    basis_ref[...] = dot(inverse_of(z2), z2)

    arrived(buf.at[:, pl.ds(0, len(PEERS) * rows), :], send_sem)
    arrived(zslots.at[pl.ds(0, len(PEERS))], zsend_sem)
    arrived(gram_other, pair_send_sem)
    arrived(gram_slots.at[pl.ds(0, len(FAR_CHIPS))], rows_send_sem)
    arrived(zz.at[pl.ds(0, len(depths))], zz_send_sem)
    arrived(gram_planes.at[pl.ds(0, len(depths))], planes_send_sem)
    for it in range(ITERS):
        arrived(zslots.at[pl.ds(0, len(PEERS))], ag_send_sem.at[it])


def project(high, low, basis_ref, core_ref, factor_ref):
    basis = basis_ref[...]
    bh, bl = split(basis)
    both = jnp.concatenate([bh, bl], axis=0)
    step = pl.program_id(0)

    @pl.when(step == 0)
    def _():
        factor_ref[...] = basis

    for i in range(core_ref.shape[0]):
        s = step * core_ref.shape[0] + i
        core_ref[i] = fold(dot(both, high[s], exact=False)) + dot(bh, low[s], exact=False)


def on_device(slab, start):
    spectra, rows, columns = slab.shape
    cols = columns // WIDE
    dma = pltpu.SemaphoreType.DMA
    vmem = pl.BlockSpec(memory_space=pltpu.VMEM)
    hbm = pl.BlockSpec(memory_space=pltpu.HBM)
    high, low, basis = pl.pallas_call(
        kernel,
        out_shape=(pltpu.VMEM((spectra, 512, cols), BF16), pltpu.VMEM((spectra, 512, cols), BF16),
                   pltpu.VMEM((64, 512), F32)),
        in_specs=[hbm, hbm],
        out_specs=(vmem, vmem, vmem),
        scratch_shapes=[
            pltpu.VMEM((64, 512), F32),
            pltpu.VMEM((spectra, 512, cols), F32),
            pltpu.VMEM((512, 512), F32),
            pltpu.VMEM((192, 512), BF16),
            pltpu.VMEM((64, 512), F32),
            pltpu.VMEM((2, WIDE // CORES, CORES, 8, 512), F32),
            pltpu.VMEM((2, WIDE // CORES, 8, 512), F32),
            pltpu.VMEM((2, WIDE // CORES, 8, 512), F32),
            pltpu.VMEM((WIDE // CORES, 2, 8, 512), F32),
            pltpu.VMEM((NZ, 2, 8, 512), F32),
            pltpu.VMEM((64, 512), F32),
            pltpu.VMEM((WIDE, 8, 128), F32),
            pltpu.VMEM((NZ, 8, 128), F32),
            pltpu.VMEM((64, 512), F32),
            pltpu.VMEM((256, 128), F32),
            dma(()), dma(()), dma(()), dma((spectra,)),
            dma(()), dma(()), dma(()), dma(()), dma((ITERS,)), dma((ITERS,)),
            dma(()), dma(()), dma(()), dma(()), dma(()), dma(()),
        ],
        compiler_params=pltpu.CompilerParams(
            collective_id=0, has_side_effects=True, vmem_limit_bytes=KERNEL_VMEM),
    )(slab, start.T)
    core, factor_t = pl.pallas_call(
        project,
        grid=(spectra // GROUP,),
        out_shape=(jax.ShapeDtypeStruct((spectra, 64, cols), F32), jax.ShapeDtypeStruct((64, 512), F32)),
        in_specs=[vmem, vmem, vmem],
        out_specs=(pl.BlockSpec((GROUP, 64, cols), lambda g: (g, 0, 0)), pl.BlockSpec((64, 512), lambda g: (0, 0))),
        compiler_params=pltpu.CompilerParams(vmem_limit_bytes=PROJECT_VMEM),
    )(high, low, basis)
    return core, factor_t.T


def solution(mesh):
    return jax.shard_map(
        on_device,
        mesh=mesh,
        in_specs=(P("narrow", "wide", None), P()),
        out_specs=(P("narrow", None, "wide"), P()),
        check_vma=False,
    )
```

```python
import jax
import jax.numpy as jnp
from jax import lax
from jax.experimental import pallas as pl
from jax.experimental.pallas import tpu as pltpu
from jax.sharding import PartitionSpec as P

MESH = pl.DeviceIdType.MESH
F32, BF16 = jnp.float32, jnp.bfloat16
ITERS = 2
AHEAD = 8
PARTS = 1
GROUP = 12
KERNEL_VMEM = 52953088
PROJECT_VMEM = 8 * 2**20
NX, NY, CORES, NZ = 4, 4, 2, 4
WIDE = NX * NY * CORES
PEERS = [(y, x, c) for y in range(NY) for x in range(NX) for c in range(CORES) if (y, x, c) != (0, 0, 0)]

FAR_FIRST = sorted(PEERS, key=lambda o: -min(o[0], NY - o[0]) - min(o[1], NX - o[1]))
FAR_CHIPS = [o for o in FAR_FIRST if o[2] == 0]


def dot(a, b, dims=((1,), (0,)), exact=True):
    precision = lax.Precision.HIGHEST if exact else None
    return lax.dot_general(a, b, (dims, ((), ())), precision=precision, preferred_element_type=F32)


def split(x):
    high = x.astype(BF16)
    return high, (x - high.astype(F32)).astype(BF16)


def inverse_factor(gram2):
    n = gram2.shape[0]
    sub = lax.broadcasted_iota(jnp.int32, (8, 2 * n), 0)
    lane = lax.broadcasted_iota(jnp.int32, (8, 2 * n), 1)
    doubled = jnp.concatenate([gram2, gram2], axis=1)
    work = [jnp.where(lane < n, doubled[8 * i:8 * i + 8], (lane - n == sub + 8 * i).astype(F32)) for i in range(n // 8)]

    def spread(x):
        return jnp.broadcast_to(x, (8, 2 * n))

    for b in range(n // 8):
        k = 8 * b
        later = range(b + 1, n // 8)
        row = [spread(work[b][t:t + 1]) for t in range(8)]
        e = [[spread(work[b][t:t + 1, k + u:k + u + 1]) for u in range(t + 1)] for t in range(8)]
        column = {i: [spread(work[i][:, k + u:k + u + 1]) for u in range(8)] for i in later}
        update = {i: 0.0 for i in later}
        for p in range(0, 8, 2):
            aa, ab, bb = e[p][p], e[p + 1][p], e[p + 1][p + 1]
            inv = 1.0 / (aa * bb - ab * ab)
            y0 = (bb * row[p] - ab * row[p + 1]) * inv
            y1 = (aa * row[p + 1] - ab * row[p]) * inv
            f = {t: ((bb * e[t][p] - ab * e[t][p + 1]) * inv, (aa * e[t][p + 1] - ab * e[t][p]) * inv)
                 for t in range(p + 2, 8)}
            for i in later:
                update[i] = update[i] + (column[i][p] * y0 + column[i][p + 1] * y1)
                for t in range(p + 2, 8):
                    column[i][t] = column[i][t] - (column[i][p] * f[t][0] + column[i][p + 1] * f[t][1])
            for t in range(p + 2, 8):
                row[t] = row[t] - (e[t][p] * y0 + e[t][p + 1] * y1)
                for u in range(p + 2, t + 1):
                    e[t][u] = e[t][u] - (e[t][p] * f[u][0] + e[t][p + 1] * f[u][1])
        for t in range(2, 8):
            work[b] = jnp.where(sub == t, row[t], work[b])
        for i in later:
            work[i] = work[i] - update[i]

    odd = sub % 2 == 1
    rows = []
    for i in range(n // 8):
        first = sub - sub % 2 + 8 * i
        before = jnp.concatenate([work[i][7:8], work[i][:7]], axis=0)
        here = jnp.where(lane == first, work[i], 0.0)
        q = jnp.sum(jnp.where(odd, here, 0.0), axis=1, keepdims=True)
        p = jnp.sum(jnp.where(odd, jnp.where(lane == first, before, 0.0), here), axis=1, keepdims=True)
        v = jnp.sum(jnp.where(jnp.logical_and(odd, lane == first + 1), work[i], 0.0), axis=1, keepdims=True)
        m = q / p
        rows.append((work[i] - m * before) / jnp.sqrt(jnp.where(odd[:, :1], v - q * m, p)))
    return jnp.concatenate(rows, axis=0)[:, n:]


def inverse_of(zt):
    c = dot(zt, zt, ((1,), (1,)))
    n = c.shape[0]
    on = lax.broadcasted_iota(jnp.int32, (n, n), 0) == lax.broadcasted_iota(jnp.int32, (n, n), 1)
    diagonal = jnp.where(on, c, 0.0)
    down = 1.0 / jnp.sqrt(jnp.sum(diagonal, axis=1, keepdims=True))
    across = 1.0 / jnp.sqrt(jnp.sum(diagonal, axis=0, keepdims=True))
    return inverse_factor((c * down) * across) * across


def fold(stacked):
    return stacked[:64] + stacked[64:]


def split3(x):
    high = x.astype(BF16)
    rest = x - high.astype(F32)
    middle = rest.astype(BF16)
    return high, middle, (rest - middle.astype(F32)).astype(BF16)


def kernel(x_ref, start_ref, high, low, basis_ref, start_buf, buf, gram, triple, zacc, gram_rows, gram_other, gram_chip, gram_slots, gram_planes,
           zsend, zslots, zz, zall, wall,
           start_sem, own_sem, send_sem, recv_sem, zsend_sem, rs_sem, zz_send_sem, zz_sem, ag_send_sem, ag_sem,
           pair_send_sem, pair_sem, rows_send_sem, rows_sem, planes_send_sem, planes_sem):
    w = lax.axis_index("wide")
    z = lax.axis_index("narrow")
    cc, xx, yy = lax.rem(w, CORES), lax.rem(w // CORES, NX), w // (CORES * NX)
    spectra, rows, cols = buf.shape[0], x_ref.shape[1], buf.shape[2]

    def peer(offset):
        y, x, c = offset
        return (lax.rem(yy + y, NY) * NX + lax.rem(xx + x, NX)) * CORES + lax.rem(cc + c, CORES)

    peers = [peer(offset) for offset in PEERS]
    far_first = [peer(offset) for offset in FAR_FIRST]
    depths = [lax.rem(z + d, NZ) for d in (2, 1, 3)]

    barrier = pltpu.get_barrier_semaphore()
    for t in far_first:
        pl.semaphore_signal(barrier, inc=1, device_id=(t, z), device_id_type=MESH)
    for d in depths:
        pl.semaphore_signal(barrier, inc=1, device_id=(w, d), device_id_type=MESH)
    my_rows = pl.ds(pl.multiple_of(w * rows, rows), rows)
    own = pltpu.make_async_copy(
        x_ref.at[:, :, pl.ds(pl.multiple_of(w * cols, cols), cols)], buf.at[:, my_rows, :], own_sem)
    own.start()
    begun = pltpu.make_async_copy(start_ref, start_buf, start_sem)
    begun.start()
    pl.semaphore_wait(barrier, len(peers) + len(depths))

    part = rows // PARTS

    def send(s):
        for r in range(PARTS):
            here = pl.ds(pl.multiple_of(w * rows + r * part, part), part)
            for t in far_first:
                pltpu.make_async_remote_copy(
                    src_ref=x_ref.at[s, pl.ds(r * part, part), pl.ds(pl.multiple_of(t * cols, cols), cols)],
                    dst_ref=buf.at[s, here, :],
                    send_sem=send_sem, recv_sem=recv_sem.at[s], device_id=(t, z), device_id_type=MESH).start()

    def arrived(ref, sem):
        pltpu.make_async_copy(ref, ref, sem).wait()

    nt = ((1,), (1,))

    def multiply(s):
        arrived(buf.at[s, pl.ds(0, len(PEERS) * rows), :], recv_sem.at[s])
        h, l = split(buf[s])
        high[s] = h
        low[s] = l
        inner = dot(triple[...], h, exact=False) + dot(triple[...], l, exact=False)
        inner = jnp.concatenate(split(inner[:64] + (inner[64:128] + inner[128:])), axis=0)
        zacc[...] += fold(dot(inner, h, nt, False) + dot(inner, l, nt, False))

    def accumulate(s):
        h, l = high[s], low[s]
        gram[...] += (dot(h, h, nt, False) + dot(h, l, nt, False)) + (dot(l, h, nt, False) + dot(l, l, nt, False))

    @pl.loop(0, AHEAD)
    def _(s):
        send(s)

    gram[...] = jnp.zeros_like(gram)
    zacc[...] = jnp.zeros_like(zacc)
    begun.wait()
    start = start_buf[...]
    triple[...] = jnp.concatenate(split3(dot(inverse_of(start), start)), axis=0)
    own.wait()

    @pl.loop(0, spectra - AHEAD)
    def _(s):
        send(s + AHEAD)
        multiply(s)
        accumulate(s)

    @pl.loop(spectra - AHEAD, spectra - 1)
    def _(s):
        multiply(s)
        accumulate(s)

    multiply(spectra - 1)

    def tile(ref, t):
        return ref.at[pl.ds(pl.multiple_of(t // 4 * 8, 8), 8), pl.ds(pl.multiple_of(lax.rem(t, 4) * 128, 128), 128)]

    def swap_planes(ref, sends, sem):
        for d in depths:
            pltpu.make_async_remote_copy(
                src_ref=ref.at[z], dst_ref=ref.at[z],
                send_sem=sends, recv_sem=sem, device_id=(w, d), device_id_type=MESH).start()

    def four_planes(ref, sem):
        arrived(ref.at[pl.ds(0, len(depths))], sem)
        return (ref[0] + ref[1]) + (ref[2] + ref[3])

    def spread(it, place, value):
        place[...] = value
        for t in far_first:
            pltpu.make_async_remote_copy(
                src_ref=place, dst_ref=place,
                send_sem=ag_send_sem.at[it], recv_sem=ag_sem.at[it], device_id=(t, z), device_id_type=MESH).start()

    zsend[...] = zacc[...]
    for t in far_first:
        pltpu.make_async_remote_copy(
            src_ref=tile(zsend, t), dst_ref=zslots.at[w],
            send_sem=zsend_sem, recv_sem=rs_sem, device_id=(t, z), device_id_type=MESH).start()
    zslots[w] = tile(zsend, w)[...]

    accumulate(spectra - 1)
    gram_rows[...] = gram[...].reshape(gram_rows.shape)
    other = peer((0, 0, 1))
    pltpu.make_async_remote_copy(
        src_ref=gram_rows.at[:, :, 1 - cc], dst_ref=gram_other,
        send_sem=pair_send_sem, recv_sem=pair_sem, device_id=(other, z), device_id_type=MESH).start()
    arrived(gram_other, pair_sem)
    gram_chip[...] = gram_rows[:, :, cc] + gram_other[...]
    chip = w // CORES
    for offset in FAR_CHIPS:
        t = peer(offset)
        pltpu.make_async_remote_copy(
            src_ref=gram_chip.at[:, t // CORES], dst_ref=gram_slots.at[chip],
            send_sem=rows_send_sem, recv_sem=rows_sem, device_id=(t, z), device_id_type=MESH).start()
    gram_slots[chip] = gram_chip[:, chip]

    arrived(zslots.at[pl.ds(0, len(PEERS))], rs_sem)
    zz[z] = jnp.sum(zslots[...], axis=0)
    swap_planes(zz, zz_send_sem, zz_sem)
    spread(0, tile(zall, w), four_planes(zz, zz_sem))

    arrived(gram_slots.at[pl.ds(0, len(FAR_CHIPS))], rows_sem)
    gram_planes[z] = jnp.sum(gram_slots[...], axis=0)
    swap_planes(gram_planes, planes_send_sem, planes_sem)

    arrived(zslots.at[pl.ds(0, len(PEERS))], ag_sem.at[0])
    z1 = zall[...]

    b1 = dot(inverse_of(z1), z1)
    mine = dot(four_planes(gram_planes, planes_sem).reshape(16, 512), b1, nt)
    spread(1, wall.at[pl.ds(pl.multiple_of(w * 8, 8), 8), :], jnp.concatenate([mine[:8], mine[8:]], axis=1))
    arrived(zslots.at[pl.ds(0, len(PEERS))], ag_sem.at[1])
    halves = wall[...].T
    z2 = jnp.concatenate([halves[:64], halves[64:]], axis=1)
    basis_ref[...] = dot(inverse_of(z2), z2)

    arrived(buf.at[:, pl.ds(0, len(PEERS) * rows), :], send_sem)
    arrived(zslots.at[pl.ds(0, len(PEERS))], zsend_sem)
    arrived(gram_other, pair_send_sem)
    arrived(gram_slots.at[pl.ds(0, len(FAR_CHIPS))], rows_send_sem)
    arrived(zz.at[pl.ds(0, len(depths))], zz_send_sem)
    arrived(gram_planes.at[pl.ds(0, len(depths))], planes_send_sem)
    for it in range(ITERS):
        arrived(zslots.at[pl.ds(0, len(PEERS))], ag_send_sem.at[it])


def project(high, low, basis_ref, core_ref, factor_ref):
    basis = basis_ref[...]
    bh, bl = split(basis)
    both = jnp.concatenate([bh, bl], axis=0)
    step = pl.program_id(0)

    @pl.when(step == 0)
    def _():
        factor_ref[...] = basis

    for i in range(core_ref.shape[0]):
        s = step * core_ref.shape[0] + i
        core_ref[i] = fold(dot(both, high[s], exact=False)) + dot(bh, low[s], exact=False)


def on_device(slab, start):
    spectra, rows, columns = slab.shape
    cols = columns // WIDE
    dma = pltpu.SemaphoreType.DMA
    vmem = pl.BlockSpec(memory_space=pltpu.VMEM)
    hbm = pl.BlockSpec(memory_space=pltpu.HBM)
    high, low, basis = pl.pallas_call(
        kernel,
        out_shape=(pltpu.VMEM((spectra, 512, cols), BF16), pltpu.VMEM((spectra, 512, cols), BF16),
                   pltpu.VMEM((64, 512), F32)),
        in_specs=[hbm, hbm],
        out_specs=(vmem, vmem, vmem),
        scratch_shapes=[
            pltpu.VMEM((64, 512), F32),
            pltpu.VMEM((spectra, 512, cols), F32),
            pltpu.VMEM((512, 512), F32),
            pltpu.VMEM((192, 512), BF16),
            pltpu.VMEM((64, 512), F32),
            pltpu.VMEM((2, WIDE // CORES, CORES, 8, 512), F32),
            pltpu.VMEM((2, WIDE // CORES, 8, 512), F32),
            pltpu.VMEM((2, WIDE // CORES, 8, 512), F32),
            pltpu.VMEM((WIDE // CORES, 2, 8, 512), F32),
            pltpu.VMEM((NZ, 2, 8, 512), F32),
            pltpu.VMEM((64, 512), F32),
            pltpu.VMEM((WIDE, 8, 128), F32),
            pltpu.VMEM((NZ, 8, 128), F32),
            pltpu.VMEM((64, 512), F32),
            pltpu.VMEM((256, 128), F32),
            dma(()), dma(()), dma(()), dma((spectra,)),
            dma(()), dma(()), dma(()), dma(()), dma((ITERS,)), dma((ITERS,)),
            dma(()), dma(()), dma(()), dma(()), dma(()), dma(()),
        ],
        compiler_params=pltpu.CompilerParams(
            collective_id=0, has_side_effects=True, vmem_limit_bytes=KERNEL_VMEM),
    )(slab, start.T)
    core, factor_t = pl.pallas_call(
        project,
        grid=(spectra // GROUP,),
        out_shape=(jax.ShapeDtypeStruct((spectra, 64, cols), F32), jax.ShapeDtypeStruct((64, 512), F32)),
        in_specs=[vmem, vmem, vmem],
        out_specs=(pl.BlockSpec((GROUP, 64, cols), lambda g: (g, 0, 0)), pl.BlockSpec((64, 512), lambda g: (0, 0))),
        compiler_params=pltpu.CompilerParams(vmem_limit_bytes=PROJECT_VMEM),
    )(high, low, basis)
    return core, factor_t.T


def solution(mesh):
    return jax.shard_map(
        on_device,
        mesh=mesh,
        in_specs=(P("narrow", "wide", None), P()),
        out_specs=(P("narrow", None, "wide"), P()),
        check_vma=False,
    )
```
